32 devices in a mesh: dp: 8 (over z, y), tensor: 4 (over x, core).
Axes of the slice: x: 2, y: 2, z: 4, core: 2. Of those that a mesh axis runs over, the one named last changes fastest.
Arguments:
- tokens: bfloat16 [16384, 768], P('dp'), may hold values from -6 to 6
- segment_ids: int32 [8, 2048], P('dp'), may hold values from 0 to 3, never falling along the last dimension, each value on 1 to 1024 neighbouring positions
- live_lengths: int32 [8], P('dp'), may hold values from 1024 to 2048
- gain_one: float32 [768], replicated, may hold values from 0.25 to 1.75
- shift_one: float32 [768], replicated, may hold values from -3 to 3
- qkv_weight: bfloat16 [3, 768, 768], P(None, None, 'tensor'), may hold values from -0.21875 to 0.21875
- out_weight: bfloat16 [768, 768], P('tensor'), may hold values from -2 to 2
- gain_two: float32 [768], replicated, may hold values from 0.25 to 1.75
- shift_two: float32 [768], replicated, may hold values from -3 to 3
- up_weight: bfloat16 [768, 3072], P(None, 'tensor'), may hold values from -0.21875 to 0.21875
- down_weight: bfloat16 [3072, 768], P('tensor'), may hold values from -0.21875 to 0.21875
- grad_out: bfloat16 [16384, 768], P('dp'), may hold values from -6 to 6
Outputs:
- output: bfloat16 [16384, 768], P('dp')
- grad_tokens: bfloat16 [16384, 768], P('dp')
- grad_gain_one: float32 [768], replicated
- grad_shift_one: float32 [768], replicated
- grad_qkv: float32 [3, 768, 768], P(None, None, 'tensor')
- grad_out_weight: float32 [768, 768], P('tensor')
- grad_gain_two: float32 [768], replicated
- grad_shift_two: float32 [768], replicated
- grad_up: float32 [768, 3072], P(None, 'tensor')
- grad_down: float32 [3072, 768], P('tensor')
The draws below stay inside these ranges and needn't reach their ends.
All inputs are finite; a program needn't handle non-finite values.
Results may differ from the reference program's by a relative error of at most 0.015.
Values may be sent and summed in bfloat16 or wider, within the bound.
No kernel may reach another device: no remote copies, remote signals or barrier semaphores. Data moves between devices by JAX's collectives and lax.ppermute only.
A program may use at most 128 MiB of HBM per device.

```python
import math
import jax
import jax.numpy as jnp
import numpy as np
from jax import lax

D = 768
HD = 64
FF = 3072
ROW_LEN = 2048
SEGS = 4
ROWS = 8
TOKENS = 16384


def touch_ends(values, key, least, high):
    longest = values.shape.index(max(values.shape))
    spots = []
    for shift in (0, 1):
        where = [jax.random.randint(jax.random.fold_in(key, axis), (), 0, length) for axis, length in enumerate(values.shape)]
        where[longest] = (where[longest] + shift) % values.shape[longest]
        spots.append(tuple(where))
    return values.at[spots[0]].set(least).at[spots[1]].set(high)


def shard_levels(own_key, dims, cuts, smallest, largest):
    factor_of, own = 1.0, jax.random.fold_in(own_key, 6)
    for dim, blocks in cuts:
        steps = jnp.exp(jax.random.uniform(jax.random.fold_in(own, dim), (blocks,), jnp.float32, smallest / len(cuts), largest / len(cuts)))
        factor_of = factor_of * jnp.repeat(steps, dims[dim] // blocks).reshape([-1 if axis == dim else 1 for axis in range(len(dims))])
    return factor_of


def length_profile(count, total, bound, slope):
    weights = [(1 << 20) // math.isqrt(grade ** slope) + 1 for grade in range(2, count + 1)]
    rest, holding = total - bound - (count - 1), [1] * (count - 1)
    while rest > 0:
        free = [i for i in range(count - 1) if holding[i] < bound]
        pool, budget = sum([weights[i] for i in free]), rest
        for i in free:
            extra = min(bound - holding[i], max(1, budget * weights[i] // pool), rest)
            holding[i] = holding[i] + extra
            rest = rest - extra
    return np.array([bound] + holding)


def uneven(rng, number_of, total, bound, skew):
    if number_of == 2:
        one = jax.random.randint(rng, (), max(1, total - bound), min(bound, total - 1) + 1)
        return jnp.stack([one, total - one])
    tallies = jnp.asarray(length_profile(number_of, total, bound, skew), jnp.int32)
    twos = (number_of - 1) // 2
    donor, sink = tallies[1:1 + 2 * twos:2], tallies[2:2 + 2 * twos:2]
    slack = jnp.minimum(donor - 1, bound - sink)
    shifted = jax.random.randint(jax.random.fold_in(rng, 1), (twos,), 0, 1 << 20) % (slack + 1)
    tallies = tallies.at[1:1 + 2 * twos:2].set(donor - shifted).at[2:2 + 2 * twos:2].set(sink + shifted)
    return tallies[jax.random.permutation(jax.random.fold_in(rng, 2), number_of)]


def noise(own_key, dims, deviation, reach, pieces=(), kind=jnp.bfloat16):
    values = jax.random.normal(own_key, dims, jnp.float32) * deviation
    if len(pieces) > 0:
        values = shard_levels(own_key, dims, pieces, -0.22, 0.18) * values
    return jnp.clip(values, min=-reach, max=reach).astype(kind)


def setup_inputs(seed: int = 0) -> dict:
    key_of = jax.random.split(jax.random.key(seed), 13)
    return {
        "tokens": noise(key_of[0], (TOKENS, D), 1.0, 6.0, ((0, 8),)),
        "segment_ids": jax.vmap(lambda own: jnp.searchsorted(jnp.cumsum(uneven(own, SEGS, ROW_LEN, ROW_LEN // 2, 2)), jnp.arange(ROW_LEN), side="right"))(jax.random.split(key_of[1], ROWS)).reshape((ROWS, ROW_LEN)).astype(jnp.int32),
        "live_lengths": touch_ends(jax.random.randint(key_of[2], (ROWS,), ROW_LEN // 2, ROW_LEN + 1), jax.random.fold_in(key_of[2], 1), ROW_LEN // 2, ROW_LEN).astype(jnp.int32),
        "gain_one": jnp.clip(1.0 + 0.15 * jax.random.normal(key_of[3], (D,), jnp.float32), 0.25, 1.75),
        "shift_one": noise(key_of[4], (D,), 0.5, 3.0, (), jnp.float32),
        "qkv_weight": noise(key_of[5], (3, D, D), D ** -0.5, 0.21875, ((2, 4),)),
        "out_weight": noise(key_of[6], (D, D), (max(D // 96, 1)) ** -0.5, 2.0, ((0, 4),)),
        "gain_two": jnp.clip(1.0 + 0.15 * jax.random.normal(key_of[7], (D,), jnp.float32), 0.25, 1.75),
        "shift_two": noise(key_of[8], (D,), 0.5, 3.0, (), jnp.float32),
        "up_weight": noise(key_of[9], (D, FF), D ** -0.5, 0.21875, ((1, 4),)),
        "down_weight": noise(key_of[10], (FF, D), (FF // 4) ** -0.5, 0.21875, ((0, 4),)),
        "grad_out": noise(key_of[11], (TOKENS, D), 1.0, 6.0, ((0, 8),)),
    }


@jax.custom_vjp
def low(v):
    return lax.optimization_barrier(v.astype(jnp.bfloat16)).astype(jnp.float32)

@jax.custom_vjp
def low_back(v):
    return v

def low_keep(v):
    return (low(v), None)

def low_pass(kept, grad):
    return (grad,)

def back_keep(v):
    return (v, None)

def back_low(kept, grad):
    return (low(grad),)
low.defvjp(low_keep, low_pass)
low_back.defvjp(back_keep, back_low)

def layer_norm(values, gain, shift):
    average = lax.optimization_barrier(jnp.mean(values, -1, keepdims=True))
    centred = values - average
    spread = lax.optimization_barrier(jnp.mean(centred * centred, -1, keepdims=True))
    return centred * lax.rsqrt(spread + 1e-05) * gain + shift

def row_attention(query, keys, values, ids, live):
    length = ids.shape[0]
    block = min(512, length)
    count = length // block
    positions = jnp.arange(length, dtype=jnp.int32)
    highest = lax.Precision.HIGHEST

    def one_block(index):
        begin = (index * block).astype(jnp.int32)
        part = lax.dynamic_slice_in_dim(query, begin, block, 0)
        own_ids = lax.dynamic_slice_in_dim(ids, begin, block, 0)
        rows_at = begin + jnp.arange(block, dtype=jnp.int32)
        allowed = (own_ids[:, None] == ids[None, :]) & ((positions[None, :] < live) | (positions[None, :] == rows_at[:, None]))
        scores = low_back(jnp.einsum('qhe,khe->hqk', part, keys, precision=highest))
        scores = jnp.where(allowed[None], scores, -1e+30)
        weights = low(jax.nn.softmax(scores, axis=-1))
        return jnp.einsum('hqk,khe->qhe', weights, values, precision=highest)
    blocks = lax.map(jax.checkpoint(one_block), jnp.arange(count, dtype=jnp.int32))
    return blocks.reshape(length, -1)

def forward(inputs, gain_one, shift_one, qkv_weight, out_weight, gain_two, shift_two, up_weight, down_weight, segment_ids, live_lengths):
    highest = lax.Precision.HIGHEST
    first = low(layer_norm(inputs, gain_one, shift_one))
    mixed = jnp.einsum('td,cde->cte', first, qkv_weight, precision=highest)
    query = low_back(low(mixed[0] * 0.125))
    keys = low_back(low(mixed[1]))
    values = low_back(low(mixed[2]))
    rows, length = segment_ids.shape
    heads = qkv_weight.shape[2] // HD

    def shaped(array):
        return array.reshape(rows, length, heads, HD)

    def one_row(item):
        return row_attention(item[0], item[1], item[2], item[3], item[4])
    attended = lax.map(one_row, (shaped(query), shaped(keys), shaped(values), segment_ids, live_lengths))
    attended = low_back(low(attended.reshape(rows * length, -1)))
    middle = inputs + low_back(jnp.dot(attended, out_weight, precision=highest))
    second = low(layer_norm(middle, gain_two, shift_two))
    pre_act = low_back(jnp.dot(second, up_weight, precision=highest))
    hidden = low(jax.nn.gelu(pre_act, approximate=False))
    return middle + low_back(jnp.dot(hidden, down_weight, precision=highest))

def reference(tokens, segment_ids, live_lengths, gain_one, shift_one, qkv_weight, out_weight, gain_two, shift_two, up_weight, down_weight, grad_out):

    def wrapped(inputs, g_one, s_one, w_qkv, w_out, g_two, s_two, w_up, w_down):
        return forward(inputs, g_one, s_one, w_qkv, w_out, g_two, s_two, w_up, w_down, segment_ids, live_lengths)
    result, backward = jax.vjp(wrapped, tokens.astype(jnp.float32), gain_one.astype(jnp.float32), shift_one.astype(jnp.float32), qkv_weight.astype(jnp.float32), out_weight.astype(jnp.float32), gain_two.astype(jnp.float32), shift_two.astype(jnp.float32), up_weight.astype(jnp.float32), down_weight.astype(jnp.float32))
    grads = backward(grad_out.astype(jnp.float32))
    return (result.astype(jnp.bfloat16), grads[0].astype(jnp.bfloat16), grads[1], grads[2], grads[3], grads[4], grads[5], grads[6], grads[7], grads[8])
```

```python
from functools import partial

import jax
import jax.numpy as jnp
from jax import lax
from jax.experimental import pallas as pl
from jax.experimental.pallas import tpu as pltpu
from jax.sharding import PartitionSpec as P

HD = 64
LANES = 128
BLK = 256
BIG = 1e30
F32 = jnp.float32
BF16 = jnp.bfloat16
VMEM = pltpu.VMEM
SMEM = pltpu.SMEM
NN = (((1,), (0,)), ((), ()))
NT = (((1,), (1,)), ((), ()))
TN = (((0,), (0,)), ((), ()))


def mm(a, b, dims=NN):
    return lax.dot_general(a, b, dims, preferred_element_type=F32)


def normalized(values):
    average = jnp.mean(values, -1, keepdims=True)
    centred = values - average
    spread = jnp.mean(centred * centred, -1, keepdims=True)
    scale = lax.rsqrt(spread + 1e-05)
    return centred * scale, scale


def norm_back(e, n, scale):
    return (e - jnp.mean(e, -1, keepdims=True) - n * jnp.mean(e * n, -1, keepdims=True)) * scale


def front_kernel(live_ref, ids_ref, x_ref, gain_ref, shift_ref, w_ref,
                 first_ref, q_ref, k_ref, v_ref, info_ref, wp_ref):
    step = pl.program_id(0)

    @pl.when(step == 0)
    def _():
        ids = ids_ref[...]
        info_ref[0] = 0
        for s in range(1, 4):
            info_ref[s] = jnp.sum(jnp.where(ids < s, 1.0, 0.0)).astype(jnp.int32)
        info_ref[4] = ids.shape[1]
        info_ref[5] = live_ref[0]
        width = w_ref.shape[2]
        wp_ref[...] = jnp.zeros_like(wp_ref)
        wp_ref[:, :, 0:width] = w_ref[...]

    n, _ = normalized(x_ref[...].astype(F32))
    first = (n * gain_ref[...] + shift_ref[...]).astype(BF16)
    first_ref[...] = first
    rows = step * BLK + lax.broadcasted_iota(jnp.int32, (BLK, LANES), 0)
    lane = lax.broadcasted_iota(jnp.int32, (BLK, LANES), 1)
    low = jnp.zeros((BLK, LANES), jnp.int32)
    high = jnp.zeros((BLK, LANES), jnp.int32)
    for s in range(4):
        low = jnp.where(lane == HD + s, info_ref[s], low)
        high = jnp.where(lane == HD + s, info_ref[s + 1], high)
    inside = (rows >= low) & (rows < high)
    flag = lane == HD + 4
    in_ids = (lane >= HD) & (lane < HD + 4)
    q_ext = jnp.where(flag | (in_ids & ~inside), -BIG, 0.0)
    k_ext = jnp.where((in_ids & inside) | (flag & (rows >= info_ref[5])), 1.0, 0.0)
    v_ext = jnp.zeros((BLK, LANES), F32)
    own = lane < HD
    for c, (ref, ext) in enumerate(((q_ref, q_ext), (k_ref, k_ext), (v_ref, v_ext))):
        res = mm(first, wp_ref[c])
        if c == 0:
            res = res * 0.125
        pair = res[:, 0:LANES]
        for h, part in enumerate((pair, pltpu.roll(pair, HD, 1), res[:, LANES:2 * LANES])):
            ref[h] = jnp.where(own, part, ext).astype(BF16)


def front(live, ids, tokens, gain, shift, weight):
    length, dim = tokens.shape
    count = length // BLK
    heads = weight.shape[2] // HD
    full = lambda *shape: pl.BlockSpec(shape, lambda i: (0,) * len(shape))
    head_spec = pl.BlockSpec((heads, BLK, LANES), lambda i: (0, i, 0))
    head_shape = jax.ShapeDtypeStruct((heads, length, LANES), BF16)
    return pl.pallas_call(
        front_kernel,
        grid=(count,),
        in_specs=[
            pl.BlockSpec(memory_space=SMEM),
            full(1, length),
            pl.BlockSpec((BLK, dim), lambda i: (i, 0)),
            full(1, dim),
            full(1, dim),
            full(*weight.shape),
        ],
        out_specs=[
            pl.BlockSpec((BLK, dim), lambda i: (i, 0)),
            head_spec, head_spec, head_spec,
            pl.BlockSpec(memory_space=SMEM),
        ],
        out_shape=[
            jax.ShapeDtypeStruct((length, dim), BF16),
            head_shape, head_shape, head_shape,
            jax.ShapeDtypeStruct((8,), jnp.int32),
        ],
        scratch_shapes=[VMEM((3, dim, 2 * LANES), BF16)],
        name="front",
    )(live, ids, tokens, gain, shift, weight)


def segment_span(info_ref, first, last):
    low, high = jnp.int32(0), info_ref[4]
    for s in range(3, 0, -1):
        at = info_ref[s]
        high = jnp.where(at > last, at, high)
    for s in range(1, 4):
        at = info_ref[s]
        low = jnp.where(at <= first, at, low)
    return low, high


def diagonal_mask(scores, base, live):
    key = lax.broadcasted_iota(jnp.int32, scores.shape, 0)
    query = lax.broadcasted_iota(jnp.int32, scores.shape, 1)
    return jnp.where((key + base >= live) & (key != query), -BIG, scores)


def drop_flag(block):
    lane = lax.broadcasted_iota(jnp.int32, block.shape, 1)
    return jnp.where(lane == HD + 4, 0.0, block.astype(F32)).astype(BF16)


def attend_kernel(info_ref, q_ref, k_ref, v_ref, att_ref, lse_ref, vt_ref, acc_ref, max_ref):
    step = pl.program_id(0)
    heads, count = vt_ref.shape[0], vt_ref.shape[1]
    extra = vt_ref.shape[2] - HD

    @pl.when(step == 0)
    def _():
        one = jnp.where(lax.broadcasted_iota(jnp.int32, (extra, BLK), 0) == 0, 1.0, 0.0).astype(BF16)

        def fill(kb, _):
            rows = pl.ds(pl.multiple_of(kb * BLK, BLK), BLK)
            for h in range(heads):
                turned = jnp.transpose(v_ref[h, rows, :].astype(F32))
                vt_ref[h, kb, 0:HD, :] = turned[0:HD].astype(BF16)
                vt_ref[h, kb, HD:HD + extra, :] = one
            return 0
        lax.fori_loop(0, count, fill, 0)

    base = step * BLK
    live = info_ref[5]
    low, high = segment_span(info_ref, base, base + BLK - 1)
    rows = pl.ds(pl.multiple_of(base, BLK), BLK)
    for h in range(heads):
        scores = diagonal_mask(mm(k_ref[h, rows, :], drop_flag(q_ref[h]), NT), base, live)
        top = jnp.max(scores, 0, keepdims=True)
        probs = jnp.exp(scores - top).astype(BF16)
        acc_ref[h] = mm(vt_ref[h, step], probs)
        max_ref[h] = top

    begin = low // BLK
    end = (jnp.minimum(high, live) + (BLK - 1)) // BLK
    total = jnp.maximum(end - begin, 0)
    total = total - jnp.where((begin <= step) & (step < end), 1, 0)

    def body(t, _):
        kb = begin + t
        kb = kb + jnp.where(kb >= step, 1, 0)
        rows = pl.ds(pl.multiple_of(kb * BLK, BLK), BLK)
        for h in range(heads):
            scores = mm(k_ref[h, rows, :], q_ref[h], NT)
            old = max_ref[h]
            top = jnp.maximum(old, jnp.max(scores, 0, keepdims=True))
            probs = jnp.exp(scores - top).astype(BF16)
            acc_ref[h] = acc_ref[h] * jnp.exp(old - top) + mm(vt_ref[h, kb], probs)
            max_ref[h] = top
        return 0

    lax.fori_loop(0, total, body, 0)
    for h in range(heads):
        sums = acc_ref[h, HD:HD + 1, :]
        att_ref[h * HD:(h + 1) * HD, :] = (acc_ref[h, 0:HD, :] / sums).astype(BF16)
        lse_ref[0, h:h + 1, :] = max_ref[h] + jnp.log(sums)


def attend(info, q, k, v):
    heads, length, _ = q.shape
    count = length // BLK
    whole = pl.BlockSpec((heads, length, LANES), lambda i: (0, 0, 0))
    return pl.pallas_call(
        attend_kernel,
        grid=(count,),
        in_specs=[
            pl.BlockSpec(memory_space=SMEM),
            pl.BlockSpec((heads, BLK, LANES), lambda i: (0, i, 0)),
            whole, whole,
        ],
        out_specs=[
            pl.BlockSpec((heads * HD, BLK), lambda i: (0, i)),
            pl.BlockSpec((1, 8, BLK), lambda i: (i, 0, 0)),
        ],
        out_shape=[
            jax.ShapeDtypeStruct((heads * HD, length), BF16),
            jax.ShapeDtypeStruct((count, 8, BLK), F32),
        ],
        scratch_shapes=[
            VMEM((heads, count, HD + 16, BLK), BF16),
            VMEM((heads, HD + 16, BLK), F32),
            VMEM((heads, 1, BLK), F32),
        ],
        name="attend",
    )(info, q, k, v)


def attend_back_kernel(half_ref, info_ref, q_ref, k_ref, v_ref, att_ref, lse_ref, own_ref, other_ref,
                       dq_ref, dk_ref, dv_ref, dot_ref, do_ref, delta_ref, dqt_ref, kt_ref, dkv_ref):
    step = pl.program_id(0)
    heads, count = dqt_ref.shape[0], dqt_ref.shape[1]
    half = count // 2

    @pl.when(step == 0)
    def _():
        def fill(t, _):
            for place, ref in ((half_ref[0], own_ref), (1 - half_ref[0], other_ref)):
                qb = place * half + t
                for h in range(heads):
                    cols = pl.ds(pl.multiple_of(t * BLK, BLK), BLK)
                    part = ref[h * HD:(h + 1) * HD, cols].astype(F32)
                    at = pl.ds(pl.multiple_of(qb * BLK, BLK), BLK)
                    att = att_ref[h * HD:(h + 1) * HD, at].astype(F32)
                    delta_ref[qb, h:h + 1, :] = jnp.sum(part * att, 0, keepdims=True)
                    padded = jnp.concatenate([part, jnp.zeros_like(part)], 0)
                    dot_ref[h, qb] = padded.astype(BF16)
                    do_ref[h, qb] = jnp.transpose(padded).astype(BF16)
                    dqt_ref[h, qb] = jnp.zeros_like(dqt_ref[h, qb])
            return 0
        lax.fori_loop(0, half, fill, 0)

    base = step * BLK
    live = info_ref[5]
    low, high = segment_span(info_ref, base, base + BLK - 1)
    for h in range(heads):
        kt_ref[h] = jnp.transpose(k_ref[h].astype(F32))[0:HD].astype(BF16)

    def pair(qb, diagonal):
        rows = pl.ds(pl.multiple_of(qb * BLK, BLK), BLK)
        for h in range(heads):
            q = q_ref[h, rows, :]
            if diagonal:
                scores = diagonal_mask(mm(k_ref[h], drop_flag(q), NT), base, live)
            else:
                scores = mm(k_ref[h], q, NT)
            probs = jnp.exp(scores - lse_ref[qb, h:h + 1, :])
            grads = probs * (mm(v_ref[h], dot_ref[h, qb]) - delta_ref[qb, h:h + 1, :])
            probs, grads = probs.astype(BF16), grads.astype(BF16)
            dv = mm(probs, do_ref[h, qb])
            dk = mm(grads, q)
            if diagonal:
                dkv_ref[0, h] = dk
                dkv_ref[1, h] = dv
            else:
                dkv_ref[0, h] += dk
                dkv_ref[1, h] += dv
            dqt_ref[h, qb] += mm(kt_ref[h], grads)

    pair(step, True)
    begin = low // BLK
    end = (high + (BLK - 1)) // BLK
    total = jnp.where(base < live, end - begin - 1, 0)

    def body(t, _):
        qb = begin + t
        pair(qb + jnp.where(qb >= step, 1, 0), False)
        return 0

    lax.fori_loop(0, total, body, 0)
    lane = lax.broadcasted_iota(jnp.int32, (BLK, LANES), 1)
    for c, ref in enumerate((dk_ref, dv_ref)):
        two = jnp.where(lane < HD, dkv_ref[c, 0], pltpu.roll(dkv_ref[c, 1], HD, 1))
        ref[:, 0:LANES] = two.astype(BF16)
        ref[:, LANES:LANES + HD] = dkv_ref[c, 2][:, 0:HD].astype(BF16)

    @pl.when(step == count - 1)
    def _():
        def drain(qb, _):
            rows = pl.ds(pl.multiple_of(qb * BLK, BLK), BLK)
            two = jnp.concatenate([dqt_ref[0, qb], dqt_ref[1, qb]], 0)
            dq_ref[rows, 0:LANES] = (jnp.transpose(two) * 0.125).astype(BF16)
            last = jnp.concatenate([dqt_ref[2, qb], dqt_ref[2, qb]], 0)
            dq_ref[rows, LANES:LANES + HD] = (jnp.transpose(last) * 0.125)[:, 0:HD].astype(BF16)
            return 0
        lax.fori_loop(0, count, drain, 0)


def attend_back(half, info, q, k, v, att, lse, own, other):
    heads, length, _ = q.shape
    count = length // BLK
    width = heads * HD
    whole = pl.BlockSpec((heads, length, LANES), lambda i: (0, 0, 0))
    block = pl.BlockSpec((heads, BLK, LANES), lambda i: (0, i, 0))
    part = jax.ShapeDtypeStruct((length, width), BF16)
    return pl.pallas_call(
        attend_back_kernel,
        grid=(count,),
        in_specs=[
            pl.BlockSpec(memory_space=SMEM),
            pl.BlockSpec(memory_space=SMEM),
            whole, block, block,
            pl.BlockSpec((width, length), lambda i: (0, 0)),
            pl.BlockSpec((count, 8, BLK), lambda i: (0, 0, 0)),
            pl.BlockSpec((width, length // 2), lambda i: (0, 0)),
            pl.BlockSpec((width, length // 2), lambda i: (0, 0)),
        ],
        out_specs=[
            pl.BlockSpec((length, width), lambda i: (0, 0)),
            pl.BlockSpec((BLK, width), lambda i: (i, 0)),
            pl.BlockSpec((BLK, width), lambda i: (i, 0)),
        ],
        out_shape=[part, part, part],
        scratch_shapes=[
            VMEM((heads, count, LANES, BLK), BF16),
            VMEM((heads, count, BLK, LANES), BF16),
            VMEM((count, 8, BLK), F32),
            VMEM((heads, count, HD, BLK), F32),
            VMEM((heads, HD, BLK), BF16),
            VMEM((2, heads, BLK, LANES), F32),
        ],
        name="attend_back",
    )(half, info, q, k, v, att, lse, own, other)


def middle_kernel(half_ref, a0, a1, a2, a3, w0, w1, w2, w3, x_ref, go_ref, gain_ref, shift_ref, up_ref, down_ref,
                  *refs):
    second_ref, hidden_ref, pre_ref, out_ref, gs_ref, mid_ref = refs[-6:]
    proj = mm(a0[...], w0[...], TN)
    for a, w in ((a1, w1), (a2, w2), (a3, w3)):
        proj = proj + mm(a[...], w[...], TN)
    middle = x_ref[...].astype(F32) + proj
    mid_ref[...] = middle
    n, _ = normalized(middle)
    second = (n * gain_ref[...] + shift_ref[...]).astype(BF16)
    second_ref[...] = second
    pre = mm(second, up_ref[...])
    phi = 0.5 + 0.5 * lax.erf(pre * 0.7071067811865476)
    hidden = (pre * phi).astype(BF16)
    hidden_ref[...] = hidden
    slope = phi + pre * (0.3989422804014327 * jnp.exp(-0.5 * pre * pre))
    grad_pre = (mm(go_ref[...], down_ref[...], NT) * slope).astype(BF16)
    pre_ref[...] = grad_pre
    out_ref[...] = (0.25 * middle + mm(hidden, down_ref[...])).astype(BF16)
    gs_ref[...] = mm(grad_pre, up_ref[...], NT).astype(BF16)


def middle_part(place, att, weights, tokens, grad_out, gain, shift, up, down, carried):
    length, dim = tokens.shape
    width = att[0].shape[0]
    steps = length // BLK // 2
    rows = pl.BlockSpec((BLK, dim), lambda i, p: (p[0] * steps + i, 0))
    local = pl.BlockSpec((BLK, dim), lambda i, p: (i, 0))
    fixed = lambda *shape: pl.BlockSpec(shape, lambda i, p: (0,) * len(shape))
    anywhere = pl.BlockSpec(memory_space=pl.ANY)
    hidden_dim = up.shape[1]
    full = lambda d: jax.ShapeDtypeStruct((length, d), BF16)
    part = lambda t: jax.ShapeDtypeStruct((length // 2, dim), t)
    first_alias = 1 + 4 + 4 + 6
    return pl.pallas_call(
        middle_kernel,
        grid_spec=pltpu.PrefetchScalarGridSpec(
            num_scalar_prefetch=1,
            grid=(steps,),
            in_specs=[pl.BlockSpec((width, BLK), lambda i, p: (0, p[0] * steps + i))] * 4
            + [fixed(width, dim)] * 4
            + [rows, rows, fixed(1, dim), fixed(1, dim), fixed(*up.shape), fixed(*down.shape)]
            + [anywhere] * len(carried),
            out_specs=[rows, rows, rows, local, local, local],
        ),
        out_shape=[full(dim), full(hidden_dim), full(hidden_dim), part(BF16), part(BF16), part(F32)],
        input_output_aliases={first_alias + i: i for i in range(len(carried))},
        name="middle",
    )(place, *att, *weights, tokens, grad_out, gain, shift, up, down, *carried)


def norm_two_kernel(half_ref, own_ref, other_ref, mid_ref, go_ref, gain_ref, w0, w1, w2, w3,
                    gm_ref, keep_ref, send_ref, sums_ref):
    @pl.when(pl.program_id(0) == 0)
    def _():
        sums_ref[...] = jnp.zeros_like(sums_ref)
    g = own_ref[...].astype(F32) + other_ref[...].astype(F32)
    n, scale = normalized(mid_ref[...])
    sums_ref[0:1, :] += jnp.sum(g * n, 0, keepdims=True)
    sums_ref[1:2, :] += jnp.sum(g, 0, keepdims=True)
    gm = (0.5 * go_ref[...].astype(F32) + norm_back(g * gain_ref[...], n, scale)).astype(BF16)
    gm_ref[...] = gm
    width = w0.shape[0]
    keep_ref[0:width, :] = mm(w0[...], gm, NT).astype(BF16)
    keep_ref[width:2 * width, :] = mm(w1[...], gm, NT).astype(BF16)
    send_ref[0:width, :] = mm(w2[...], gm, NT).astype(BF16)
    send_ref[width:2 * width, :] = mm(w3[...], gm, NT).astype(BF16)


def norm_two(place, own, other, middle, grad_out, gain, weights):
    rows, dim = own.shape
    width = weights[0].shape[0]
    steps = rows // BLK
    local = pl.BlockSpec((BLK, dim), lambda i, p: (i, 0))
    fixed = lambda *shape: pl.BlockSpec(shape, lambda i, p: (0,) * len(shape))
    cols = pl.BlockSpec((2 * width, BLK), lambda i, p: (0, i))
    return pl.pallas_call(
        norm_two_kernel,
        grid_spec=pltpu.PrefetchScalarGridSpec(
            num_scalar_prefetch=1,
            grid=(steps,),
            in_specs=[local, local, local, pl.BlockSpec((BLK, dim), lambda i, p: (p[0] * steps + i, 0)), fixed(1, dim)]
            + [fixed(width, dim)] * 4,
            out_specs=[local, cols, cols, fixed(8, dim)],
        ),
        out_shape=[
            jax.ShapeDtypeStruct((rows, dim), BF16),
            jax.ShapeDtypeStruct((2 * width, rows), BF16),
            jax.ShapeDtypeStruct((2 * width, rows), BF16),
            jax.ShapeDtypeStruct((8, dim), F32),
        ],
        name="norm_two",
    )(place, own, other, middle, grad_out, gain, *weights)


def first_grad_kernel(place_ref, dq_ref, dk_ref, dv_ref, w_ref, out_ref):
    total = mm(dq_ref[...], w_ref[0], NT)
    total = total + mm(dk_ref[...], w_ref[1], NT)
    out_ref[...] = (total + mm(dv_ref[...], w_ref[2], NT)).astype(BF16)


def first_grad(place, dq, dk, dv, weight):
    length, width = dq.shape
    dim = weight.shape[1]
    steps = length // BLK // 2
    rows = pl.BlockSpec((BLK, width), lambda i, p: (p[0] * steps + i, 0))
    return pl.pallas_call(
        first_grad_kernel,
        grid_spec=pltpu.PrefetchScalarGridSpec(
            num_scalar_prefetch=1,
            grid=(steps,),
            in_specs=[rows, rows, rows, pl.BlockSpec(weight.shape, lambda i, p: (0, 0, 0))],
            out_specs=pl.BlockSpec((BLK, dim), lambda i, p: (i, 0)),
        ),
        out_shape=jax.ShapeDtypeStruct((length // 2, dim), BF16),
        name="first_grad",
    )(place, dq, dk, dv, weight)


def norm_one_kernel(place_ref, own_ref, other_ref, x_ref, gm_ref, gain_ref, out_ref, sums_ref):
    @pl.when(pl.program_id(0) == 0)
    def _():
        sums_ref[...] = jnp.zeros_like(sums_ref)
    g = own_ref[...].astype(F32) + other_ref[...].astype(F32)
    n, scale = normalized(x_ref[...].astype(F32))
    sums_ref[0:1, :] += jnp.sum(g * n, 0, keepdims=True)
    sums_ref[1:2, :] += jnp.sum(g, 0, keepdims=True)
    out_ref[...] = (gm_ref[...].astype(F32) + norm_back(g * gain_ref[...], n, scale)).astype(BF16)


def norm_one(place, own, other, tokens, gm, gain):
    rows, dim = own.shape
    steps = rows // BLK
    local = pl.BlockSpec((BLK, dim), lambda i, p: (i, 0))
    fixed = lambda *shape: pl.BlockSpec(shape, lambda i, p: (0,) * len(shape))
    return pl.pallas_call(
        norm_one_kernel,
        grid_spec=pltpu.PrefetchScalarGridSpec(
            num_scalar_prefetch=1,
            grid=(steps,),
            in_specs=[local, local, pl.BlockSpec((BLK, dim), lambda i, p: (p[0] * steps + i, 0)), local, fixed(1, dim)],
            out_specs=[local, fixed(8, dim)],
        ),
        out_shape=[jax.ShapeDtypeStruct((rows, dim), BF16), jax.ShapeDtypeStruct((8, dim), F32)],
        name="norm_one",
    )(place, own, other, tokens, gm, gain)


def swap(value, distance):
    return lax.ppermute(value, "tensor", [(t, t ^ distance) for t in range(4)])


def add(a, b):
    return a.astype(F32) + b.astype(F32)


def both_halves(core, mine):
    other = swap(mine, 1)
    rows = mine.shape[0]
    full = jnp.zeros((2 * rows, mine.shape[1]), mine.dtype)
    full = lax.dynamic_update_slice(full, mine, (core * rows, 0))
    return lax.dynamic_update_slice(full, other, ((1 - core) * rows, 0))


def local(
    tokens,
    segment_ids,
    live_lengths,
    gain_one,
    shift_one,
    qkv_weight,
    out_weight,
    gain_two,
    shift_two,
    up_weight,
    down_weight,
    grad_out,
):
    core = lax.axis_index("tensor") % 2
    mine = jnp.full((1,), core, jnp.int32)
    theirs = 1 - mine
    row = lambda v: v.reshape(1, -1)
    w_sib = swap(out_weight, 1)
    w_far = swap(out_weight, 2)
    w_diag = swap(w_far, 1)
    weights = (out_weight, w_sib, w_far, w_diag)

    first, q, k, v, info = front(live_lengths, segment_ids, tokens, row(gain_one), row(shift_one), qkv_weight)
    att, lse = attend(info, q, k, v)
    att_far = swap(att, 2)
    att_sib = swap(att, 1)
    att_diag = swap(att_far, 1)
    atts = (att, att_sib, att_far, att_diag)

    args = (atts, weights, tokens, grad_out, row(gain_two), row(shift_two), up_weight, down_weight)
    second, hidden, grad_pre, out_theirs, gs_theirs, _ = middle_part(theirs, *args, ())
    gs_got = swap(gs_theirs, 1)
    second, hidden, grad_pre, out_mine, gs_mine, middle = middle_part(mine, *args, (second, hidden, grad_pre))
    grad_mid, keep, send, sums_two = norm_two(mine, gs_mine, gs_got, middle, grad_out, row(gain_two), weights)
    got = swap(send, 2)
    width = out_weight.shape[0]
    grad_att_own = add(keep[:width], got[:width]).astype(BF16)
    grad_att_sib = add(keep[width:], got[width:]).astype(BF16)
    grad_att_other = swap(grad_att_sib, 1)

    dq, dk, dv = attend_back(mine, info, q, k, v, att, lse, grad_att_own, grad_att_other)
    gf_got = swap(first_grad(theirs, dq, dk, dv, qkv_weight), 1)
    gf_mine = first_grad(mine, dq, dk, dv, qkv_weight)
    partial_tokens, sums_one = norm_one(mine, gf_mine, gf_got, tokens, grad_mid, row(gain_one))
    grad_tokens = both_halves(core, add(partial_tokens, swap(partial_tokens, 2)).astype(BF16))

    out_half = add(out_mine, swap(out_theirs, 1)).astype(BF16)
    output = both_halves(core, add(out_half, swap(out_half, 2)).astype(BF16))

    grad_down = jnp.einsum("tf,td->fd", hidden, grad_out, preferred_element_type=F32)
    grad_up = jnp.einsum("td,tf->df", second, grad_pre, preferred_element_type=F32)
    rows = tokens.shape[0] // 2
    pieces = [
        jnp.dot(lax.dynamic_slice_in_dim(a, core * rows, rows, 1), grad_mid, preferred_element_type=F32) for a in atts
    ]
    pieces = [p.astype(BF16) for p in pieces]
    own = add(pieces[0], swap(pieces[1], 1))
    far = add(pieces[2], swap(pieces[3], 1))
    grad_out_weight = own + swap(far.astype(BF16), 2).astype(F32)
    grad_qkv = jnp.stack([jnp.einsum("td,te->de", first, g, preferred_element_type=F32) for g in (dq, dk, dv)])

    grads = lax.psum(tuple(g.astype(BF16) for g in (grad_up, grad_down)), "dp")
    grad_up, grad_down = (g.astype(F32) for g in grads)
    grads = lax.psum(tuple(g.astype(BF16) for g in (grad_qkv, grad_out_weight)), "dp")
    grad_qkv, grad_out_weight = (g.astype(F32) for g in grads)
    sums = lax.psum(jnp.concatenate([sums_one[0:2], sums_two[0:2]], 0), ("dp", "tensor"))
    return (
        output,
        grad_tokens,
        sums[0],
        sums[1],
        grad_qkv,
        grad_out_weight,
        sums[2],
        sums[3],
        grad_up,
        grad_down,
    )


def solution(mesh):
    in_specs = (
        P("dp", None),
        P("dp", None),
        P("dp"),
        P(),
        P(),
        P(None, None, "tensor"),
        P("tensor", None),
        P(),
        P(),
        P(None, "tensor"),
        P("tensor", None),
        P("dp", None),
    )
    out_specs = (
        P("dp", None),
        P("dp", None),
        P(),
        P(),
        P(None, None, "tensor"),
        P("tensor", None),
        P(),
        P(),
        P(None, "tensor"),
        P("tensor", None),
    )
    return jax.shard_map(local, mesh=mesh, in_specs=in_specs, out_specs=out_specs, check_vma=False)
```

```python
from functools import partial

import jax
import jax.numpy as jnp
from jax import lax
from jax.experimental import pallas as pl
from jax.experimental.pallas import tpu as pltpu
from jax.sharding import PartitionSpec as P

HD = 64
LANES = 128
BLK = 256
BIG = 1e30
ZERO, MINE, THEIRS = 3, 4, 5
F32 = jnp.float32
BF16 = jnp.bfloat16
VMEM = pltpu.VMEM
SMEM = pltpu.SMEM
NN = (((1,), (0,)), ((), ()))
NT = (((1,), (1,)), ((), ()))
TN = (((0,), (0,)), ((), ()))


def mm(a, b, dims=NN):
    return lax.dot_general(a, b, dims, preferred_element_type=F32)


def normalized(values):
    average = jnp.mean(values, -1, keepdims=True)
    centred = values - average
    spread = jnp.mean(centred * centred, -1, keepdims=True)
    scale = lax.rsqrt(spread + 1e-05)
    return centred * scale, scale


def norm_back(e, n, scale):
    return (e - jnp.mean(e, -1, keepdims=True) - n * jnp.mean(e * n, -1, keepdims=True)) * scale


def cost(us):
    return pl.CostEstimate(flops=int(us), bytes_accessed=int(us), transcendentals=0)


def front_kernel(live_ref, ids_ref, x_ref, norm_ref, w_ref,
                 first_ref, q_ref, k_ref, v_ref, info_ref, wp_ref):
    step = pl.program_id(0)

    @pl.when(step == 0)
    def _():
        ids = ids_ref[...]
        info_ref[0] = 0
        for s in range(1, 4):
            info_ref[s] = jnp.sum(jnp.where(ids < s, 1.0, 0.0)).astype(jnp.int32)
        info_ref[4] = ids.shape[1]
        info_ref[5] = live_ref[0]
        width = w_ref.shape[1]
        for c in range(3):
            wp_ref[c, 0:width, :] = w_ref[c]
            wp_ref[c, width:, :] = jnp.zeros_like(wp_ref[c, width:, :])

    n, _ = normalized(x_ref[...].astype(F32))
    first = (n * norm_ref[0:1, :] + norm_ref[1:2, :]).astype(BF16)
    first_ref[...] = first
    rows = step * BLK + lax.broadcasted_iota(jnp.int32, (BLK, LANES), 0)
    lane = lax.broadcasted_iota(jnp.int32, (BLK, LANES), 1)
    low = jnp.zeros((BLK, LANES), jnp.int32)
    high = jnp.zeros((BLK, LANES), jnp.int32)
    for s in range(4):
        low = jnp.where(lane == HD + s, info_ref[s], low)
        high = jnp.where(lane == HD + s, info_ref[s + 1], high)
    inside = (rows >= low) & (rows < high)
    flag = lane == HD + 4
    in_ids = (lane >= HD) & (lane < HD + 4)
    q_ext = jnp.where(flag | (in_ids & ~inside), -BIG, 0.0)
    k_ext = jnp.where((in_ids & inside) | (flag & (rows >= info_ref[5])), 1.0, 0.0)
    v_ext = jnp.zeros((BLK, LANES), F32)
    own = lane < HD
    for c, (ref, ext) in enumerate(((q_ref, q_ext), (k_ref, k_ext), (v_ref, v_ext))):
        res = mm(first, wp_ref[c], NT)
        if c == 0:
            res = res * 0.125
        pair = res[:, 0:LANES]
        for h, part in enumerate((pair, pltpu.roll(pair, HD, 1), res[:, LANES:2 * LANES])):
            ref[h] = jnp.where(own, part, ext).astype(BF16)


def front(live, ids, tokens, norms, weight):
    length, dim = tokens.shape
    count = length // BLK
    heads = weight.shape[1] // HD
    full = lambda *shape: pl.BlockSpec(shape, lambda i: (0,) * len(shape))
    head_spec = pl.BlockSpec((heads, BLK, LANES), lambda i: (0, i, 0))
    head_shape = jax.ShapeDtypeStruct((heads, length, LANES), BF16)
    return pl.pallas_call(
        front_kernel,
        grid=(count,),
        in_specs=[
            pl.BlockSpec(memory_space=SMEM),
            full(1, length),
            pl.BlockSpec((BLK, dim), lambda i: (i, 0)),
            full(*norms.shape),
            full(*weight.shape),
        ],
        out_specs=[
            pl.BlockSpec((BLK, dim), lambda i: (i, 0)),
            head_spec, head_spec, head_spec,
            pl.BlockSpec(memory_space=SMEM),
        ],
        out_shape=[
            jax.ShapeDtypeStruct((length, dim), BF16),
            head_shape, head_shape, head_shape,
            jax.ShapeDtypeStruct((8,), jnp.int32),
        ],
        scratch_shapes=[VMEM((3, 2 * LANES, dim), BF16)],
        cost_estimate=cost(10),
        name="front",
    )(live, ids, tokens, norms, weight)


def segment_span(info_ref, first, last):
    low, high = jnp.int32(0), info_ref[4]
    for s in range(3, 0, -1):
        at = info_ref[s]
        high = jnp.where(at > last, at, high)
    for s in range(1, 4):
        at = info_ref[s]
        low = jnp.where(at <= first, at, low)
    return low, high


def diagonal_mask(scores, base, live):
    key = lax.broadcasted_iota(jnp.int32, scores.shape, 0)
    query = lax.broadcasted_iota(jnp.int32, scores.shape, 1)
    return jnp.where((key + base >= live) & (key != query), -BIG, scores)


def drop_flag(block):
    lane = lax.broadcasted_iota(jnp.int32, block.shape, 1)
    return jnp.where(lane == HD + 4, 0.0, block.astype(F32)).astype(BF16)


def tile_rows(tile):
    return pl.ds(pl.multiple_of(tile * BLK, BLK), BLK)


def attend_kernel(info_ref, q_ref, k_ref, v_ref, att_ref, lse_ref, vt_ref, acc_ref, max_ref, s_ref):
    step = pl.program_id(0)
    heads, count = vt_ref.shape[0], vt_ref.shape[1]
    extra = vt_ref.shape[2] - HD

    @pl.when(step == 0)
    def _():
        one = jnp.where(lax.broadcasted_iota(jnp.int32, (extra, BLK), 0) == 0, 1.0, 0.0).astype(BF16)
        def fill(kb, _):
            for h in range(heads):
                turned = jnp.transpose(v_ref[h, tile_rows(kb), :].astype(F32))
                vt_ref[h, kb, 0:HD, :] = turned[0:HD].astype(BF16)
                vt_ref[h, kb, HD:HD + extra, :] = one
            return 0
        lax.fori_loop(0, count, fill, 0)
    base = step * BLK
    live = info_ref[5]
    low, high = segment_span(info_ref, base, base + BLK - 1)
    begin = low // BLK
    end = (jnp.minimum(high, live) + (BLK - 1)) // BLK
    total = jnp.maximum(end - begin, 0)
    total = total - jnp.where((begin <= step) & (step < end), 1, 0)
    at = lambda t: begin + t + jnp.where(begin + t >= step, 1, 0)
    part = lambda x: jnp.max(x.reshape(BLK // 8, 8, BLK), 0)
    odd = total % 2 == 1
    skip = jnp.where(odd, 1, 0)

    def score(h, kb):
        a = mm(k_ref[h, tile_rows(kb), :], q_ref[h], NT)
        s_ref[h, kb] = a
        return part(a)

    def diag(h):
        a = diagonal_mask(mm(k_ref[h, tile_rows(step), :], drop_flag(q_ref[h]), NT), base, live)
        s_ref[h, step] = a
        return part(a)

    @pl.when(odd)
    def _():
        for h in range(heads):
            max_ref[h] = jnp.maximum(diag(h), score(h, at(0)))

    @pl.when(~odd)
    def _():
        for h in range(heads):
            max_ref[h] = diag(h)

    def one(t, _):
        ka, kb = at(skip + 2 * t), at(skip + 2 * t + 1)
        for h in range(heads):
            max_ref[h] = jnp.maximum(max_ref[h], jnp.maximum(score(h, ka), score(h, kb)))
        return 0
    lax.fori_loop(0, (total - skip) // 2, one, 0)
    for h in range(heads):
        max_ref[h] = jnp.broadcast_to(jnp.max(max_ref[h], 0, keepdims=True), (8, BLK))
    pv = lambda h, kb: mm(vt_ref[h, kb], jnp.exp(s_ref[h, kb] - max_ref[h, 0:1]).astype(BF16))

    @pl.when(odd)
    def _():
        for h in range(heads):
            acc_ref[h] = pv(h, step) + pv(h, at(0))

    @pl.when(~odd)
    def _():
        for h in range(heads):
            acc_ref[h] = pv(h, step)

    def two(t, _):
        ka, kb = at(skip + 2 * t), at(skip + 2 * t + 1)
        for h in range(heads):
            acc_ref[h] += pv(h, ka) + pv(h, kb)
        return 0
    lax.fori_loop(0, (total - skip) // 2, two, 0)
    for h in range(heads):
        sums = acc_ref[h, HD:HD + 1, :]
        att_ref[h * HD:(h + 1) * HD, :] = (acc_ref[h, 0:HD, :] / sums).astype(BF16)
        lse_ref[0, h:h + 1, :] = max_ref[h, 0:1] + jnp.log(sums)


def attend(info, q, k, v):
    heads, length, _ = q.shape
    count = length // BLK
    whole = pl.BlockSpec((heads, length, LANES), lambda i: (0, 0, 0))
    return pl.pallas_call(
        attend_kernel,
        grid=(count,),
        in_specs=[
            pl.BlockSpec(memory_space=SMEM),
            pl.BlockSpec((heads, BLK, LANES), lambda i: (0, i, 0)),
            whole, whole,
        ],
        out_specs=[
            pl.BlockSpec((heads * HD, BLK), lambda i: (0, i)),
            pl.BlockSpec((1, 8, BLK), lambda i: (i, 0, 0)),
        ],
        out_shape=[
            jax.ShapeDtypeStruct((heads * HD, length), BF16),
            jax.ShapeDtypeStruct((count, 8, BLK), F32),
        ],
        scratch_shapes=[
            VMEM((heads, count, HD + 16, BLK), BF16),
            VMEM((heads, HD + 16, BLK), F32),
            VMEM((heads, 8, BLK), F32),
            VMEM((heads, count, BLK, BLK), F32),
        ],
        cost_estimate=cost(20),
        name="attend",
    )(info, q, k, v)


def attend_back_kernel(half_ref, info_ref, q_ref, k_ref, v_ref, att_ref, lse_ref, own_ref, other_ref,
                       dq_ref, dk_ref, dv_ref, dot_ref, do_ref, delta_ref, dqt_ref, kt_ref, dkv_ref,
                       p_ref, g_ref):
    step = pl.program_id(0)
    heads, count = dqt_ref.shape[0], dqt_ref.shape[1]
    half = count // 2

    @pl.when(step == 0)
    def _():
        def fill(t, _):
            for place, ref in ((half_ref[MINE], own_ref), (1 - half_ref[MINE], other_ref)):
                qb = place * half + t
                for h in range(heads):
                    cols = pl.ds(pl.multiple_of(t * BLK, BLK), BLK)
                    part = ref[h * HD:(h + 1) * HD, cols].astype(F32)
                    at = pl.ds(pl.multiple_of(qb * BLK, BLK), BLK)
                    att = att_ref[h * HD:(h + 1) * HD, at].astype(F32)
                    delta_ref[qb, h:h + 1, :] = jnp.sum(part * att, 0, keepdims=True)
                    padded = jnp.concatenate([part, jnp.zeros_like(part)], 0)
                    dot_ref[h, qb] = padded.astype(BF16)
                    do_ref[h, qb] = jnp.transpose(padded).astype(BF16)
                    dqt_ref[h, qb] = jnp.zeros_like(dqt_ref[h, qb])
            return 0
        lax.fori_loop(0, half, fill, 0)

    base = step * BLK
    live = info_ref[5]
    low, high = segment_span(info_ref, base, base + BLK - 1)
    for h in range(heads):
        kt_ref[h] = jnp.transpose(k_ref[h].astype(F32))[0:HD].astype(BF16)
        dkv_ref[0, h] = jnp.zeros_like(dkv_ref[0, h])
        dkv_ref[1, h] = jnp.zeros_like(dkv_ref[1, h])

    def produce(qb, diagonal):
        for h in range(heads):
            q = q_ref[h, tile_rows(qb), :]
            if diagonal:
                scores = diagonal_mask(mm(k_ref[h], drop_flag(q), NT), base, live)
            else:
                scores = mm(k_ref[h], q, NT)
            probs = jnp.exp(scores - lse_ref[qb, h:h + 1, :])
            p_ref[h] = probs.astype(BF16)
            g_ref[h] = (probs * (mm(v_ref[h], dot_ref[h, qb]) - delta_ref[qb, h:h + 1, :])).astype(BF16)

    def consume(qb):
        for h in range(heads):
            dkv_ref[1, h] += mm(p_ref[h], do_ref[h, qb])
            dkv_ref[0, h] += mm(g_ref[h], q_ref[h, tile_rows(qb), :])
            dqt_ref[h, qb] += mm(kt_ref[h], g_ref[h])

    begin = low // BLK
    end = (high + (BLK - 1)) // BLK
    total = jnp.where(base < live, end - begin - 1, 0)
    produce(step, True)

    def body(t, last):
        consume(last)
        qb = begin + t
        qb = qb + jnp.where(qb >= step, 1, 0)
        produce(qb, False)
        return qb

    consume(lax.fori_loop(0, total, body, step))
    lane = lax.broadcasted_iota(jnp.int32, (BLK, LANES), 1)
    for c, ref in enumerate((dk_ref, dv_ref)):
        two = jnp.where(lane < HD, dkv_ref[c, 0], pltpu.roll(dkv_ref[c, 1], HD, 1))
        ref[:, 0:LANES] = two.astype(BF16)
        ref[:, LANES:LANES + HD] = dkv_ref[c, 2][:, 0:HD].astype(BF16)

    @pl.when(step == count - 1)
    def _():
        def drain(qb, _):
            rows = pl.ds(pl.multiple_of(qb * BLK, BLK), BLK)
            two = jnp.concatenate([dqt_ref[0, qb], dqt_ref[1, qb]], 0)
            dq_ref[rows, 0:LANES] = (jnp.transpose(two) * 0.125).astype(BF16)
            last = jnp.concatenate([dqt_ref[2, qb], dqt_ref[2, qb]], 0)
            dq_ref[rows, LANES:LANES + HD] = (jnp.transpose(last) * 0.125)[:, 0:HD].astype(BF16)
            return 0
        lax.fori_loop(0, count, drain, 0)


def attend_back(half, info, q, k, v, att, lse, own, other):
    heads, length, _ = q.shape
    count = length // BLK
    width = heads * HD
    whole = pl.BlockSpec((heads, length, LANES), lambda i: (0, 0, 0))
    block = pl.BlockSpec((heads, BLK, LANES), lambda i: (0, i, 0))
    part = jax.ShapeDtypeStruct((length, width), BF16)
    return pl.pallas_call(
        attend_back_kernel,
        grid=(count,),
        in_specs=[
            pl.BlockSpec(memory_space=SMEM),
            pl.BlockSpec(memory_space=SMEM),
            whole, block, block,
            pl.BlockSpec((width, length), lambda i: (0, 0)),
            pl.BlockSpec((count, 8, BLK), lambda i: (0, 0, 0)),
            pl.BlockSpec((width, length // 2), lambda i: (0, 0)),
            pl.BlockSpec((width, length // 2), lambda i: (0, 0)),
        ],
        out_specs=[
            pl.BlockSpec((length, width), lambda i: (0, 0)),
            pl.BlockSpec((BLK, width), lambda i: (i, 0)),
            pl.BlockSpec((BLK, width), lambda i: (i, 0)),
        ],
        out_shape=[part, part, part],
        scratch_shapes=[
            VMEM((heads, count, LANES, BLK), BF16),
            VMEM((heads, count, BLK, LANES), BF16),
            VMEM((count, 8, BLK), F32),
            VMEM((heads, count, HD, BLK), F32),
            VMEM((heads, HD, BLK), BF16),
            VMEM((2, heads, BLK, LANES), F32),
            VMEM((heads, BLK, BLK), BF16),
            VMEM((heads, BLK, BLK), BF16),
        ],
        cost_estimate=cost(28),
        name="attend_back",
    )(half, info, q, k, v, att, lse, own, other)


def middle_kernel(half_ref, a0, a1, a2, a3, w0, w1, w2, w3, x_ref, go_ref, norm_ref, up_ref, down_ref,
                  *refs):
    second_ref, hidden_ref, pre_ref, out_ref, gs_ref, mid_ref = refs[-6:]
    proj = mm(a0[...], w0[...], TN)
    for a, w in ((a1, w1), (a2, w2), (a3, w3)):
        proj = proj + mm(a[...], w[...], TN)
    middle = x_ref[...].astype(F32) + proj
    mid_ref[...] = middle
    n, _ = normalized(middle)
    second = (n * norm_ref[2:3, :] + norm_ref[3:4, :]).astype(BF16)
    second_ref[...] = second
    pre = mm(second, up_ref[...])
    phi = 0.5 + 0.5 * lax.erf(pre * 0.7071067811865476)
    hidden = (pre * phi).astype(BF16)
    hidden_ref[...] = hidden
    slope = phi + pre * (0.3989422804014327 * jnp.exp(-0.5 * pre * pre))
    grad_pre = (mm(go_ref[...], down_ref[...], NT) * slope).astype(BF16)
    pre_ref[...] = grad_pre
    out_ref[...] = (0.25 * middle + mm(hidden, down_ref[...])).astype(BF16)
    gs_ref[...] = mm(grad_pre, up_ref[...], NT).astype(BF16)


def middle_part(table, at, att, weights, tokens, grad_out, norms, up, down, carried):
    length, dim = tokens.shape
    width = att[0].shape[0]
    steps = length // BLK // 2
    rows = pl.BlockSpec((BLK, dim), lambda i, p: (p[at] * steps + i, 0))
    local = pl.BlockSpec((BLK, dim), lambda i, p: (i, 0))
    fixed = lambda *shape: pl.BlockSpec(shape, lambda i, p: (0,) * len(shape))
    anywhere = pl.BlockSpec(memory_space=pl.ANY)
    hidden_dim = up.shape[1]
    full = lambda d: jax.ShapeDtypeStruct((length, d), BF16)
    part = lambda t: jax.ShapeDtypeStruct((length // 2, dim), t)
    first_alias = 1 + 4 + 4 + 5
    return pl.pallas_call(
        middle_kernel,
        grid_spec=pltpu.PrefetchScalarGridSpec(
            num_scalar_prefetch=1,
            grid=(steps,),
            in_specs=[pl.BlockSpec((width, BLK), lambda i, p: (0, p[at] * steps + i))] * 4
            + [fixed(width, dim)] * 4
            + [rows, rows, fixed(*norms.shape), fixed(*up.shape), fixed(*down.shape)]
            + [anywhere] * len(carried),
            out_specs=[rows, rows, rows, local, local, local],
        ),
        out_shape=[full(dim), full(hidden_dim), full(hidden_dim), part(BF16), part(BF16), part(F32)],
        input_output_aliases={first_alias + i: i for i in range(len(carried))},
        cost_estimate=cost(14),
        name="middle",
    )(table, *att, *weights, tokens, grad_out, norms, up, down, *carried)


def norm_two_kernel(half_ref, own_ref, other_ref, mid_ref, go_ref, norm_ref, w0, w1, w2, w3,
                    gm_ref, keep_ref, send_ref, sums_ref):
    @pl.when(pl.program_id(0) == 0)
    def _():
        sums_ref[...] = jnp.zeros_like(sums_ref)
    g = own_ref[...].astype(F32) + other_ref[...].astype(F32)
    n, scale = normalized(mid_ref[...])
    sums_ref[0:1, :] += jnp.sum(g * n, 0, keepdims=True)
    sums_ref[1:2, :] += jnp.sum(g, 0, keepdims=True)
    gm = (0.5 * go_ref[...].astype(F32) + norm_back(g * norm_ref[2:3, :], n, scale)).astype(BF16)
    gm_ref[...] = gm
    width = w0.shape[0]
    keep_ref[0:width, :] = mm(w0[...], gm, NT).astype(BF16)
    keep_ref[width:2 * width, :] = mm(w1[...], gm, NT).astype(BF16)
    send_ref[0:width, :] = mm(w2[...], gm, NT).astype(BF16)
    send_ref[width:2 * width, :] = mm(w3[...], gm, NT).astype(BF16)


def norm_two(table, own, other, middle, grad_out, norms, weights):
    rows, dim = own.shape
    width = weights[0].shape[0]
    steps = rows // BLK
    local = pl.BlockSpec((BLK, dim), lambda i, p: (i, 0))
    fixed = lambda *shape: pl.BlockSpec(shape, lambda i, p: (0,) * len(shape))
    cols = pl.BlockSpec((2 * width, BLK), lambda i, p: (0, i))
    return pl.pallas_call(
        norm_two_kernel,
        grid_spec=pltpu.PrefetchScalarGridSpec(
            num_scalar_prefetch=1,
            grid=(steps,),
            in_specs=[local, local, local, pl.BlockSpec((BLK, dim), lambda i, p: (p[MINE] * steps + i, 0)),
                      fixed(*norms.shape)]
            + [fixed(width, dim)] * 4,
            out_specs=[local, cols, cols, fixed(8, dim)],
        ),
        out_shape=[
            jax.ShapeDtypeStruct((rows, dim), BF16),
            jax.ShapeDtypeStruct((2 * width, rows), BF16),
            jax.ShapeDtypeStruct((2 * width, rows), BF16),
            jax.ShapeDtypeStruct((8, dim), F32),
        ],
        cost_estimate=cost(8),
        name="norm_two",
    )(table, own, other, middle, grad_out, norms, *weights)


def first_total(dq_ref, dk_ref, dv_ref, w_ref):
    total = mm(dq_ref[...], w_ref[0])
    total = total + mm(dk_ref[...], w_ref[1])
    return total + mm(dv_ref[...], w_ref[2])


def first_grad_kernel(place_ref, dq_ref, dk_ref, dv_ref, w_ref, out_ref):
    out_ref[...] = first_total(dq_ref, dk_ref, dv_ref, w_ref).astype(BF16)


def first_grad(table, at, dq, dk, dv, weight):
    length, width = dq.shape
    dim = weight.shape[2]
    steps = length // BLK // 2
    rows = pl.BlockSpec((BLK, width), lambda i, p: (p[at] * steps + i, 0))
    return pl.pallas_call(
        first_grad_kernel,
        grid_spec=pltpu.PrefetchScalarGridSpec(
            num_scalar_prefetch=1,
            grid=(steps,),
            in_specs=[rows, rows, rows, pl.BlockSpec(weight.shape, lambda i, p: (0, 0, 0))],
            out_specs=pl.BlockSpec((BLK, dim), lambda i, p: (i, 0)),
        ),
        out_shape=jax.ShapeDtypeStruct((length // 2, dim), BF16),
        cost_estimate=cost(4),
        name="first_grad",
    )(table, dq, dk, dv, weight)


def norm_one_kernel(place_ref, dq_ref, dk_ref, dv_ref, w_ref, other_ref, x_ref, gm_ref, norm_ref, sums_two_ref,
                    out_ref, sums_ref):
    @pl.when(pl.program_id(0) == 0)
    def _():
        sums_ref[...] = sums_two_ref[...]
    g = first_total(dq_ref, dk_ref, dv_ref, w_ref) + other_ref[...].astype(F32)
    n, scale = normalized(x_ref[...].astype(F32))
    sums_ref[2:3, :] += jnp.sum(g * n, 0, keepdims=True)
    sums_ref[3:4, :] += jnp.sum(g, 0, keepdims=True)
    out_ref[...] = (gm_ref[...].astype(F32) + norm_back(g * norm_ref[0:1, :], n, scale)).astype(BF16)


def norm_one(table, dq, dk, dv, weight, other, tokens, gm, norms, sums_two):
    rows, dim = other.shape
    width = dq.shape[1]
    steps = rows // BLK
    local = pl.BlockSpec((BLK, dim), lambda i, p: (i, 0))
    placed = lambda d: pl.BlockSpec((BLK, d), lambda i, p: (p[MINE] * steps + i, 0))
    fixed = lambda *shape: pl.BlockSpec(shape, lambda i, p: (0,) * len(shape))
    return pl.pallas_call(
        norm_one_kernel,
        grid_spec=pltpu.PrefetchScalarGridSpec(
            num_scalar_prefetch=1,
            grid=(steps,),
            in_specs=[placed(width)] * 3 + [fixed(*weight.shape), local, placed(dim), local, fixed(*norms.shape),
                                            fixed(8, dim)],
            out_specs=[local, fixed(8, dim)],
        ),
        out_shape=[jax.ShapeDtypeStruct((rows, dim), BF16), jax.ShapeDtypeStruct((8, dim), F32)],
        cost_estimate=cost(10),
        name="norm_one",
    )(table, dq, dk, dv, weight, other, tokens, gm, norms, sums_two)


def fold_kernel(picks, cuts, table_ref, *refs):
    count = len(picks)
    ins, outs = refs[:2 * count], refs[2 * count:]
    for i in range(count):
        got, own = ins[2 * i], ins[2 * i + 1]
        base = table_ref[picks[i]] * got.shape[0]
        if cuts is None:
            at = pl.ds(pl.multiple_of(base, got.shape[0]), got.shape[0])
            outs[i][...] = (got[...].astype(F32) + own[at, :].astype(F32)).astype(BF16)
            continue
        keep, send = outs[2 * i], outs[2 * i + 1]
        rows = keep.shape[0]
        cut = table_ref[cuts[i]]
        for ref, half in ((keep, cut), (send, 1 - cut)):
            here = pl.ds(pl.multiple_of(half * rows, rows), rows)
            there = pl.ds(pl.multiple_of(base + half * rows, rows), rows)
            ref[...] = (got[here, :].astype(F32) + own[there, :].astype(F32)).astype(BF16)


def in_vmem(count):
    return [pl.BlockSpec(memory_space=VMEM)] * count


def fold(table, picks, cuts, pairs):
    outs, args = [], []
    for got, own in pairs:
        rows, dim = got.shape
        outs += [jax.ShapeDtypeStruct((rows, dim), BF16)] if cuts is None else [
            jax.ShapeDtypeStruct((rows // 2, dim), BF16)] * 2
        args += [got, own]
    res = pl.pallas_call(
        partial(fold_kernel, picks, cuts),
        in_specs=[pl.BlockSpec(memory_space=SMEM)] + in_vmem(len(args)),
        out_specs=in_vmem(len(outs)),
        out_shape=outs,
        cost_estimate=cost(1),
        name="fold",
    )(table, *args)
    return res if cuts is None else ([res[0], res[2]], [res[1], res[3]])


def join_kernel(bits, table_ref, *refs):
    count = len(bits)
    for i in range(count):
        own, got, out = refs[2 * i], refs[2 * i + 1], refs[2 * count + i]
        rows = own.shape[0]
        for ref, half in ((own, table_ref[bits[i]]), (got, 1 - table_ref[bits[i]])):
            out[pl.ds(pl.multiple_of(half * rows, rows), rows), :] = ref[...].astype(out.dtype)


def join(table, bits, pairs):
    outs, args = [], []
    for own, got in pairs:
        outs.append(jax.ShapeDtypeStruct((2 * own.shape[0], own.shape[1]), own.dtype))
        args += [own, got]
    return pl.pallas_call(
        partial(join_kernel, bits),
        in_specs=[pl.BlockSpec(memory_space=SMEM)] + in_vmem(len(args)),
        out_specs=in_vmem(len(outs)),
        out_shape=outs,
        cost_estimate=cost(1),
        name="join",
    )(table, *args)


def last_join_kernel(bits, table_ref, *refs):
    count = len(bits)
    for i in range(count):
        own, got, out = refs[2 * i], refs[2 * i + 1], refs[2 * count + i]
        for ref, half in ((own, table_ref[bits[i]]), (got, 1 - table_ref[bits[i]])):
            @pl.when(pl.program_id(0) == half)
            def _():
                out[...] = ref[...].astype(F32)


def last_join(table, bits, pairs):
    outs, specs, args = [], [], []
    for own, got in pairs:
        rows, dim = own.shape
        outs.append(jax.ShapeDtypeStruct((2 * rows, dim), F32))
        specs.append(pl.BlockSpec((rows, dim), lambda i: (i, 0)))
        args += [own, got]
    return pl.pallas_call(
        partial(last_join_kernel, bits),
        grid=(2,),
        in_specs=[pl.BlockSpec(memory_space=SMEM)] + in_vmem(len(args)),
        out_specs=specs,
        out_shape=outs,
        cost_estimate=cost(2),
        name="last_join",
    )(table, *args)


def dp_swap(value, distance):
    return lax.ppermute(value, "dp", [(d, d ^ distance) for d in range(lax.axis_size("dp"))])


ORDERS = ((0, 1, 2), (1, 2, 0))


def place_table():
    core = lax.axis_index("tensor") % 2
    code = lax.axis_index("dp") % 8 + 16 * core + 32 * (1 - core)
    return (code // jnp.array([1, 2, 4, 8, 16, 32, 64, 128], jnp.int32)) % 2


def dp_sum_pair(table, a, b, extra, held):
    if lax.axis_size("dp") != 8:
        a, b, extra = lax.psum((a, b, extra), "dp")
        return a.astype(F32), b.astype(F32), extra, held
    index = lax.axis_index("dp")
    rows = a.shape[0] // 2
    own = [a, b]
    send = [
        lax.dynamic_slice_in_dim(v, (1 - (index >> o[0]) % 2) * rows, rows, 0) for v, o in zip(own, ORDERS)
    ]
    for step in range(3):
        got = [dp_swap(v, 1 << o[step]) for v, o in zip(send, ORDERS)]
        extra = extra + dp_swap(extra, 1 << step)
        extra, got = lax.optimization_barrier((extra, got))
        picks = [o[0] if step == 0 else ZERO for o in ORDERS]
        pairs = list(zip(got, own))
        if step == 2:
            own = fold(table, picks, None, pairs)
            break
        own, send = fold(table, picks, [o[step + 1] for o in ORDERS], pairs)
    own, held = lax.optimization_barrier((own, held))
    for step in (2, 1, 0):
        got = [dp_swap(v, 1 << o[step]) for v, o in zip(own, ORDERS)]
        own = (join if step else last_join)(table, [o[step] for o in ORDERS], list(zip(own, got)))
    return *own, extra, held


def swap(value, distance):
    return lax.ppermute(value, "tensor", [(t, t ^ distance) for t in range(4)])


def add(a, b):
    return a.astype(F32) + b.astype(F32)


def both_halves(core, mine):
    other = swap(mine, 1)
    rows = mine.shape[0]
    full = jnp.zeros((2 * rows, mine.shape[1]), mine.dtype)
    full = lax.dynamic_update_slice(full, mine, (core * rows, 0))
    return lax.dynamic_update_slice(full, other, ((1 - core) * rows, 0))


def local(
    tokens,
    segment_ids,
    live_lengths,
    gain_one,
    shift_one,
    qkv_weight,
    out_weight,
    gain_two,
    shift_two,
    up_weight,
    down_weight,
    grad_out,
):
    core = lax.axis_index("tensor") % 2
    table = place_table()
    norms = jnp.stack([gain_one, shift_one, gain_two, shift_two])
    qkv = jnp.swapaxes(qkv_weight, 1, 2)
    w_far = swap(out_weight, 2)
    w_sib = swap(out_weight, 1)
    w_diag = swap(w_far, 1)

    first, q, k, v, info = front(live_lengths, segment_ids, tokens, norms, qkv)
    att, lse = attend(info, q, k, v)
    att, w_sib, w_far, w_diag = lax.optimization_barrier((att, w_sib, w_far, w_diag))
    weights = (out_weight, w_sib, w_far, w_diag)
    att_far = swap(att, 2)
    att_sib = swap(att, 1)
    att_diag = swap(att_far, 1)
    atts = (att, att_sib, att_far, att_diag)

    args = (atts, weights, tokens, grad_out, norms, up_weight, down_weight)
    second, hidden, grad_pre, out_theirs, gs_theirs, _ = middle_part(table, THEIRS, *args, ())
    gs_got = swap(gs_theirs, 1)
    second, hidden, grad_pre, out_mine, gs_mine, middle = middle_part(table, MINE, *args, (second, hidden, grad_pre))
    grad_mid, keep, send, sums_two = norm_two(table, gs_mine, gs_got, middle, grad_out, norms, weights)
    send, second, hidden, grad_pre = lax.optimization_barrier((send, second, hidden, grad_pre))
    got = swap(send, 2)
    width = out_weight.shape[0]
    out_half = add(out_mine, swap(out_theirs, 1)).astype(BF16)

    grad_down = jnp.einsum("tf,td->fd", hidden, grad_out, preferred_element_type=F32).astype(BF16)
    grad_up = jnp.einsum("td,tf->df", second, grad_pre, preferred_element_type=F32).astype(BF16)
    rows = tokens.shape[0] // 2
    pieces = [
        jnp.dot(lax.dynamic_slice_in_dim(a, core * rows, rows, 1), grad_mid, preferred_element_type=F32) for a in atts
    ]
    pieces = [p.astype(BF16) for p in pieces]
    own = add(pieces[0], swap(pieces[1], 1))
    far = add(pieces[2], swap(pieces[3], 1)).astype(BF16)

    got, out_half, far = lax.optimization_barrier((got, out_half, far))
    keep, grad_down, grad_up = lax.optimization_barrier((keep, grad_down, grad_up))
    out_far = swap(out_half, 2)
    grad_down, grad_up = (g.astype(F32) for g in lax.psum((grad_down, grad_up), "dp"))
    grad_att_own = add(keep[:width], got[:width]).astype(BF16)
    grad_att_sib = add(keep[width:], got[width:]).astype(BF16)
    grad_att_other = swap(grad_att_sib, 1)
    grad_out_weight = (own + swap(far, 2).astype(F32)).astype(BF16)

    dq, dk, dv = attend_back(table, info, q, k, v, att, lse, grad_att_own, grad_att_other)
    gf_got = swap(first_grad(table, THEIRS, dq, dk, dv, qkv), 1)
    partial_tokens, sums = norm_one(table, dq, dk, dv, qkv, gf_got, tokens, grad_mid, norms, sums_two)
    partial_tokens, out_far = lax.optimization_barrier((partial_tokens, out_far))
    tokens_far = swap(partial_tokens, 2)
    output = both_halves(core, add(out_half, out_far).astype(BF16))
    sums = sums + swap(sums, 1)
    turn = lambda g: jnp.einsum("te,td->ed", g, first, preferred_element_type=F32).astype(BF16)
    grad_qk, grad_vo, sums, tokens_far = dp_sum_pair(
        table, jnp.concatenate([turn(dq), turn(dk)], 0), jnp.concatenate([turn(dv), grad_out_weight], 0), sums, tokens_far
    )
    sums, tokens_far = lax.optimization_barrier((sums, tokens_far))
    sums = sums + swap(sums, 2)
    grad_tokens = both_halves(core, add(partial_tokens, tokens_far).astype(BF16))
    grad_qkv = jnp.concatenate([grad_qk, grad_vo[:width]], 0).reshape(3, width, -1).swapaxes(1, 2)
    grad_out_weight = grad_vo[width:]
    return (
        output,
        grad_tokens,
        sums[2],
        sums[3],
        grad_qkv,
        grad_out_weight,
        sums[0],
        sums[1],
        grad_up,
        grad_down,
    )


def solution(mesh):
    in_specs = (
        P("dp", None),
        P("dp", None),
        P("dp"),
        P(),
        P(),
        P(None, None, "tensor"),
        P("tensor", None),
        P(),
        P(),
        P(None, "tensor"),
        P("tensor", None),
        P("dp", None),
    )
    out_specs = (
        P("dp", None),
        P("dp", None),
        P(),
        P(),
        P(None, None, "tensor"),
        P("tensor", None),
        P(),
        P(),
        P(None, "tensor"),
        P("tensor", None),
    )
    return jax.shard_map(local, mesh=mesh, in_specs=in_specs, out_specs=out_specs, check_vma=False)
```

```python
from functools import partial

import jax
import jax.numpy as jnp
from jax import lax
from jax.experimental import pallas as pl
from jax.experimental.pallas import tpu as pltpu
from jax.sharding import PartitionSpec as P

HD = 64
LANES = 128
BLK = 256
BIG = 1e30
ZERO, MINE, THEIRS = 3, 4, 5
F32 = jnp.float32
BF16 = jnp.bfloat16
VMEM = pltpu.VMEM
SMEM = pltpu.SMEM
NN = (((1,), (0,)), ((), ()))
NT = (((1,), (1,)), ((), ()))
TN = (((0,), (0,)), ((), ()))


def mm(a, b, dims=NN):
    return lax.dot_general(a, b, dims, preferred_element_type=F32)


def normalized(values):
    average = jnp.mean(values, -1, keepdims=True)
    centred = values - average
    spread = jnp.mean(centred * centred, -1, keepdims=True)
    scale = lax.rsqrt(spread + 1e-05)
    return centred * scale, scale


def norm_back(e, n, scale):
    return (e - jnp.mean(e, -1, keepdims=True) - n * jnp.mean(e * n, -1, keepdims=True)) * scale


def cost(us):
    return pl.CostEstimate(flops=int(us), bytes_accessed=int(us), transcendentals=0)


def front_kernel(live_ref, ids_ref, x_ref, norm_ref, w_ref,
                 first_ref, q_ref, k_ref, v_ref, info_ref, wp_ref):
    step = pl.program_id(0)

    @pl.when(step == 0)
    def _():
        ids = ids_ref[...]
        info_ref[0] = 0
        for s in range(1, 4):
            info_ref[s] = jnp.sum(jnp.where(ids < s, 1.0, 0.0)).astype(jnp.int32)
        info_ref[4] = ids.shape[1]
        info_ref[5] = live_ref[0]
        width = w_ref.shape[1]
        for c in range(3):
            wp_ref[c, 0:width, :] = w_ref[c]
            wp_ref[c, width:, :] = jnp.zeros_like(wp_ref[c, width:, :])

    n, _ = normalized(x_ref[...].astype(F32))
    first = (n * norm_ref[0:1, :] + norm_ref[1:2, :]).astype(BF16)
    first_ref[...] = first
    rows = step * BLK + lax.broadcasted_iota(jnp.int32, (BLK, LANES), 0)
    lane = lax.broadcasted_iota(jnp.int32, (BLK, LANES), 1)
    low = jnp.zeros((BLK, LANES), jnp.int32)
    high = jnp.zeros((BLK, LANES), jnp.int32)
    for s in range(4):
        low = jnp.where(lane == HD + s, info_ref[s], low)
        high = jnp.where(lane == HD + s, info_ref[s + 1], high)
    inside = (rows >= low) & (rows < high)
    flag = lane == HD + 4
    in_ids = (lane >= HD) & (lane < HD + 4)
    q_ext = jnp.where(flag | (in_ids & ~inside), -BIG, 0.0)
    k_ext = jnp.where((in_ids & inside) | (flag & (rows >= info_ref[5])), 1.0, 0.0)
    v_ext = jnp.zeros((BLK, LANES), F32)
    own = lane < HD
    for c, (ref, ext) in enumerate(((q_ref, q_ext), (k_ref, k_ext), (v_ref, v_ext))):
        res = mm(first, wp_ref[c], NT)
        if c == 0:
            res = res * 0.125
        pair = res[:, 0:LANES]
        for h, part in enumerate((pair, pltpu.roll(pair, HD, 1), res[:, LANES:2 * LANES])):
            ref[h] = jnp.where(own, part, ext).astype(BF16)


def front(live, ids, tokens, norms, weight):
    length, dim = tokens.shape
    count = length // BLK
    heads = weight.shape[1] // HD
    full = lambda *shape: pl.BlockSpec(shape, lambda i: (0,) * len(shape))
    head_spec = pl.BlockSpec((heads, BLK, LANES), lambda i: (0, i, 0))
    head_shape = jax.ShapeDtypeStruct((heads, length, LANES), BF16)
    return pl.pallas_call(
        front_kernel,
        grid=(count,),
        in_specs=[
            pl.BlockSpec(memory_space=SMEM),
            full(1, length),
            pl.BlockSpec((BLK, dim), lambda i: (i, 0)),
            full(*norms.shape),
            full(*weight.shape),
        ],
        out_specs=[
            pl.BlockSpec((BLK, dim), lambda i: (i, 0)),
            head_spec, head_spec, head_spec,
            pl.BlockSpec(memory_space=SMEM),
        ],
        out_shape=[
            jax.ShapeDtypeStruct((length, dim), BF16),
            head_shape, head_shape, head_shape,
            jax.ShapeDtypeStruct((8,), jnp.int32),
        ],
        scratch_shapes=[VMEM((3, 2 * LANES, dim), BF16)],
        cost_estimate=cost(10),
        name="front",
    )(live, ids, tokens, norms, weight)


def segment_span(info_ref, first, last):
    low, high = jnp.int32(0), info_ref[4]
    for s in range(3, 0, -1):
        at = info_ref[s]
        high = jnp.where(at > last, at, high)
    for s in range(1, 4):
        at = info_ref[s]
        low = jnp.where(at <= first, at, low)
    return low, high


def diagonal_mask(scores, base, live):
    key = lax.broadcasted_iota(jnp.int32, scores.shape, 0)
    query = lax.broadcasted_iota(jnp.int32, scores.shape, 1)
    return jnp.where((key + base >= live) & (key != query), -BIG, scores)


def drop_flag(block):
    lane = lax.broadcasted_iota(jnp.int32, block.shape, 1)
    return jnp.where(lane == HD + 4, 0.0, block.astype(F32)).astype(BF16)


def tile_rows(tile):
    return pl.ds(pl.multiple_of(tile * BLK, BLK), BLK)


def attend_kernel(info_ref, q_ref, k_ref, v_ref, att_ref, lse_ref, vt_ref, acc_ref, max_ref, s_ref):
    step = pl.program_id(0)
    heads, count = vt_ref.shape[0], vt_ref.shape[1]
    extra = vt_ref.shape[2] - HD

    @pl.when(step == 0)
    def _():
        one = jnp.where(lax.broadcasted_iota(jnp.int32, (extra, BLK), 0) == 0, 1.0, 0.0).astype(BF16)
        def fill(kb, _):
            for h in range(heads):
                turned = jnp.transpose(v_ref[h, tile_rows(kb), :].astype(F32))
                vt_ref[h, kb, 0:HD, :] = turned[0:HD].astype(BF16)
                vt_ref[h, kb, HD:HD + extra, :] = one
            return 0
        lax.fori_loop(0, count, fill, 0)
    base = step * BLK
    live = info_ref[5]
    low, high = segment_span(info_ref, base, base + BLK - 1)
    begin = low // BLK
    end = (jnp.minimum(high, live) + (BLK - 1)) // BLK
    total = jnp.maximum(end - begin, 0)
    total = total - jnp.where((begin <= step) & (step < end), 1, 0)
    at = lambda t: begin + t + jnp.where(begin + t >= step, 1, 0)
    part = lambda x: jnp.max(x.reshape(BLK // 8, 8, BLK), 0)
    odd = total % 2 == 1
    skip = jnp.where(odd, 1, 0)

    def score(h, kb):
        a = mm(k_ref[h, tile_rows(kb), :], q_ref[h], NT)
        s_ref[h, kb] = a
        return part(a)

    def diag(h):
        a = diagonal_mask(mm(k_ref[h, tile_rows(step), :], drop_flag(q_ref[h]), NT), base, live)
        s_ref[h, step] = a
        return part(a)

    @pl.when(odd)
    def _():
        for h in range(heads):
            max_ref[h] = jnp.maximum(diag(h), score(h, at(0)))

    @pl.when(~odd)
    def _():
        for h in range(heads):
            max_ref[h] = diag(h)

    def one(t, _):
        ka, kb = at(skip + 2 * t), at(skip + 2 * t + 1)
        for h in range(heads):
            max_ref[h] = jnp.maximum(max_ref[h], jnp.maximum(score(h, ka), score(h, kb)))
        return 0
    lax.fori_loop(0, (total - skip) // 2, one, 0)
    for h in range(heads):
        max_ref[h] = jnp.broadcast_to(jnp.max(max_ref[h], 0, keepdims=True), (8, BLK))
    pv = lambda h, kb: mm(vt_ref[h, kb], jnp.exp(s_ref[h, kb] - max_ref[h, 0:1]).astype(BF16))

    @pl.when(odd)
    def _():
        for h in range(heads):
            acc_ref[h] = pv(h, step) + pv(h, at(0))

    @pl.when(~odd)
    def _():
        for h in range(heads):
            acc_ref[h] = pv(h, step)

    def two(t, _):
        ka, kb = at(skip + 2 * t), at(skip + 2 * t + 1)
        for h in range(heads):
            acc_ref[h] += pv(h, ka) + pv(h, kb)
        return 0
    lax.fori_loop(0, (total - skip) // 2, two, 0)
    for h in range(heads):
        sums = acc_ref[h, HD:HD + 1, :]
        att_ref[h * HD:(h + 1) * HD, :] = (acc_ref[h, 0:HD, :] / sums).astype(BF16)
        lse_ref[0, h:h + 1, :] = max_ref[h, 0:1] + jnp.log(sums)


def attend(info, q, k, v):
    heads, length, _ = q.shape
    count = length // BLK
    whole = pl.BlockSpec((heads, length, LANES), lambda i: (0, 0, 0))
    return pl.pallas_call(
        attend_kernel,
        grid=(count,),
        in_specs=[
            pl.BlockSpec(memory_space=SMEM),
            pl.BlockSpec((heads, BLK, LANES), lambda i: (0, i, 0)),
            whole, whole,
        ],
        out_specs=[
            pl.BlockSpec((heads * HD, BLK), lambda i: (0, i)),
            pl.BlockSpec((1, 8, BLK), lambda i: (i, 0, 0)),
        ],
        out_shape=[
            jax.ShapeDtypeStruct((heads * HD, length), BF16),
            jax.ShapeDtypeStruct((count, 8, BLK), F32),
        ],
        scratch_shapes=[
            VMEM((heads, count, HD + 16, BLK), BF16),
            VMEM((heads, HD + 16, BLK), F32),
            VMEM((heads, 8, BLK), F32),
            VMEM((heads, count, BLK, BLK), F32),
        ],
        cost_estimate=cost(20),
        name="attend",
    )(info, q, k, v)


def attend_back_kernel(half_ref, info_ref, q_ref, k_ref, v_ref, att_ref, lse_ref, own_ref, other_ref,
                       dq_ref, dk_ref, dv_ref, dot_ref, do_ref, delta_ref, dqt_ref, kt_ref, dkv_ref,
                       p_ref, g_ref):
    step = pl.program_id(0)
    heads, count = dqt_ref.shape[0], dqt_ref.shape[1]
    half = count // 2

    @pl.when(step == 0)
    def _():
        def fill(t, _):
            for place, ref in ((half_ref[MINE], own_ref), (1 - half_ref[MINE], other_ref)):
                qb = place * half + t
                for h in range(heads):
                    cols = pl.ds(pl.multiple_of(t * BLK, BLK), BLK)
                    part = ref[h * HD:(h + 1) * HD, cols].astype(F32)
                    at = pl.ds(pl.multiple_of(qb * BLK, BLK), BLK)
                    att = att_ref[h * HD:(h + 1) * HD, at].astype(F32)
                    delta_ref[qb, h:h + 1, :] = jnp.sum(part * att, 0, keepdims=True)
                    padded = jnp.concatenate([part, jnp.zeros_like(part)], 0)
                    dot_ref[h, qb] = padded.astype(BF16)
                    do_ref[h, qb] = jnp.transpose(padded).astype(BF16)
                    dqt_ref[h, qb] = jnp.zeros_like(dqt_ref[h, qb])
            return 0
        lax.fori_loop(0, half, fill, 0)

    base = step * BLK
    live = info_ref[5]
    low, high = segment_span(info_ref, base, base + BLK - 1)
    for h in range(heads):
        kt_ref[h] = jnp.transpose(k_ref[h].astype(F32))[0:HD].astype(BF16)
        dkv_ref[0, h] = jnp.zeros_like(dkv_ref[0, h])
        dkv_ref[1, h] = jnp.zeros_like(dkv_ref[1, h])

    def produce(qb, diagonal):
        for h in range(heads):
            q = q_ref[h, tile_rows(qb), :]
            if diagonal:
                scores = diagonal_mask(mm(k_ref[h], drop_flag(q), NT), base, live)
            else:
                scores = mm(k_ref[h], q, NT)
            probs = jnp.exp(scores - lse_ref[qb, h:h + 1, :])
            p_ref[h] = probs.astype(BF16)
            g_ref[h] = (probs * (mm(v_ref[h], dot_ref[h, qb]) - delta_ref[qb, h:h + 1, :])).astype(BF16)

    def consume(qb):
        for h in range(heads):
            dkv_ref[1, h] += mm(p_ref[h], do_ref[h, qb])
            dkv_ref[0, h] += mm(g_ref[h], q_ref[h, tile_rows(qb), :])
            dqt_ref[h, qb] += mm(kt_ref[h], g_ref[h])

    begin = low // BLK
    end = (high + (BLK - 1)) // BLK
    total = jnp.where(base < live, end - begin - 1, 0)
    produce(step, True)

    def body(t, last):
        consume(last)
        qb = begin + t
        qb = qb + jnp.where(qb >= step, 1, 0)
        produce(qb, False)
        return qb

    consume(lax.fori_loop(0, total, body, step))
    lane = lax.broadcasted_iota(jnp.int32, (BLK, LANES), 1)
    for c, ref in enumerate((dk_ref, dv_ref)):
        two = jnp.where(lane < HD, dkv_ref[c, 0], pltpu.roll(dkv_ref[c, 1], HD, 1))
        ref[:, 0:LANES] = two.astype(BF16)
        ref[:, LANES:LANES + HD] = dkv_ref[c, 2][:, 0:HD].astype(BF16)

    @pl.when(step == count - 1)
    def _():
        def drain(qb, _):
            rows = pl.ds(pl.multiple_of(qb * BLK, BLK), BLK)
            two = jnp.concatenate([dqt_ref[0, qb], dqt_ref[1, qb]], 0)
            dq_ref[rows, 0:LANES] = (jnp.transpose(two) * 0.125).astype(BF16)
            last = jnp.concatenate([dqt_ref[2, qb], dqt_ref[2, qb]], 0)
            dq_ref[rows, LANES:LANES + HD] = (jnp.transpose(last) * 0.125)[:, 0:HD].astype(BF16)
            return 0
        lax.fori_loop(0, count, drain, 0)


def attend_back(half, info, q, k, v, att, lse, own, other):
    heads, length, _ = q.shape
    count = length // BLK
    width = heads * HD
    whole = pl.BlockSpec((heads, length, LANES), lambda i: (0, 0, 0))
    block = pl.BlockSpec((heads, BLK, LANES), lambda i: (0, i, 0))
    part = jax.ShapeDtypeStruct((length, width), BF16)
    return pl.pallas_call(
        attend_back_kernel,
        grid=(count,),
        in_specs=[
            pl.BlockSpec(memory_space=SMEM),
            pl.BlockSpec(memory_space=SMEM),
            whole, block, block,
            pl.BlockSpec((width, length), lambda i: (0, 0)),
            pl.BlockSpec((count, 8, BLK), lambda i: (0, 0, 0)),
            pl.BlockSpec((width, length // 2), lambda i: (0, 0)),
            pl.BlockSpec((width, length // 2), lambda i: (0, 0)),
        ],
        out_specs=[
            pl.BlockSpec((length, width), lambda i: (0, 0)),
            pl.BlockSpec((BLK, width), lambda i: (i, 0)),
            pl.BlockSpec((BLK, width), lambda i: (i, 0)),
        ],
        out_shape=[part, part, part],
        scratch_shapes=[
            VMEM((heads, count, LANES, BLK), BF16),
            VMEM((heads, count, BLK, LANES), BF16),
            VMEM((count, 8, BLK), F32),
            VMEM((heads, count, HD, BLK), F32),
            VMEM((heads, HD, BLK), BF16),
            VMEM((2, heads, BLK, LANES), F32),
            VMEM((heads, BLK, BLK), BF16),
            VMEM((heads, BLK, BLK), BF16),
        ],
        cost_estimate=cost(10**11),
        name="attend_back",
    )(half, info, q, k, v, att, lse, own, other)


def middle_kernel(half_ref, a0, a1, a2, a3, w0, w1, w2, w3, x_ref, go_ref, norm_ref, up_ref, down_ref,
                  *refs):
    second_ref, hidden_ref, pre_ref, out_ref, gs_ref, mid_ref = refs[-6:]
    proj = mm(a0[...], w0[...], TN)
    for a, w in ((a1, w1), (a2, w2), (a3, w3)):
        proj = proj + mm(a[...], w[...], TN)
    middle = x_ref[...].astype(F32) + proj
    mid_ref[...] = middle
    n, _ = normalized(middle)
    second = (n * norm_ref[2:3, :] + norm_ref[3:4, :]).astype(BF16)
    second_ref[...] = second
    pre = mm(second, up_ref[...])
    phi = 0.5 + 0.5 * lax.erf(pre * 0.7071067811865476)
    hidden = (pre * phi).astype(BF16)
    hidden_ref[...] = hidden
    slope = phi + pre * (0.3989422804014327 * jnp.exp(-0.5 * pre * pre))
    grad_pre = (mm(go_ref[...], down_ref[...], NT) * slope).astype(BF16)
    pre_ref[...] = grad_pre
    out_ref[...] = (0.25 * middle + mm(hidden, down_ref[...])).astype(BF16)
    gs_ref[...] = mm(grad_pre, up_ref[...], NT).astype(BF16)


def middle_part(table, at, att, weights, tokens, grad_out, norms, up, down, carried):
    length, dim = tokens.shape
    width = att[0].shape[0]
    steps = length // BLK // 2
    rows = pl.BlockSpec((BLK, dim), lambda i, p: (p[at] * steps + i, 0))
    local = pl.BlockSpec((BLK, dim), lambda i, p: (i, 0))
    fixed = lambda *shape: pl.BlockSpec(shape, lambda i, p: (0,) * len(shape))
    anywhere = pl.BlockSpec(memory_space=pl.ANY)
    hidden_dim = up.shape[1]
    full = lambda d: jax.ShapeDtypeStruct((length, d), BF16)
    part = lambda t: jax.ShapeDtypeStruct((length // 2, dim), t)
    first_alias = 1 + 4 + 4 + 5
    return pl.pallas_call(
        middle_kernel,
        grid_spec=pltpu.PrefetchScalarGridSpec(
            num_scalar_prefetch=1,
            grid=(steps,),
            in_specs=[pl.BlockSpec((width, BLK), lambda i, p: (0, p[at] * steps + i))] * 4
            + [fixed(width, dim)] * 4
            + [rows, rows, fixed(*norms.shape), fixed(*up.shape), fixed(*down.shape)]
            + [anywhere] * len(carried),
            out_specs=[rows, rows, rows, local, local, local],
        ),
        out_shape=[full(dim), full(hidden_dim), full(hidden_dim), part(BF16), part(BF16), part(F32)],
        input_output_aliases={first_alias + i: i for i in range(len(carried))},
        cost_estimate=cost(14),
        name="middle",
    )(table, *att, *weights, tokens, grad_out, norms, up, down, *carried)


def norm_two_kernel(half_ref, own_ref, other_ref, mid_ref, go_ref, norm_ref, w0, w1, w2, w3,
                    gm_ref, keep_ref, send_ref, sums_ref):
    @pl.when(pl.program_id(0) == 0)
    def _():
        sums_ref[...] = jnp.zeros_like(sums_ref)
    g = own_ref[...].astype(F32) + other_ref[...].astype(F32)
    n, scale = normalized(mid_ref[...])
    sums_ref[0:1, :] += jnp.sum(g * n, 0, keepdims=True)
    sums_ref[1:2, :] += jnp.sum(g, 0, keepdims=True)
    gm = (0.5 * go_ref[...].astype(F32) + norm_back(g * norm_ref[2:3, :], n, scale)).astype(BF16)
    gm_ref[...] = gm
    width = w0.shape[0]
    keep_ref[0:width, :] = mm(w0[...], gm, NT).astype(BF16)
    keep_ref[width:2 * width, :] = mm(w1[...], gm, NT).astype(BF16)
    send_ref[0:width, :] = mm(w2[...], gm, NT).astype(BF16)
    send_ref[width:2 * width, :] = mm(w3[...], gm, NT).astype(BF16)


def norm_two(table, own, other, middle, grad_out, norms, weights):
    rows, dim = own.shape
    width = weights[0].shape[0]
    steps = rows // BLK
    local = pl.BlockSpec((BLK, dim), lambda i, p: (i, 0))
    fixed = lambda *shape: pl.BlockSpec(shape, lambda i, p: (0,) * len(shape))
    cols = pl.BlockSpec((2 * width, BLK), lambda i, p: (0, i))
    return pl.pallas_call(
        norm_two_kernel,
        grid_spec=pltpu.PrefetchScalarGridSpec(
            num_scalar_prefetch=1,
            grid=(steps,),
            in_specs=[local, local, local, pl.BlockSpec((BLK, dim), lambda i, p: (p[MINE] * steps + i, 0)),
                      fixed(*norms.shape)]
            + [fixed(width, dim)] * 4,
            out_specs=[local, cols, cols, fixed(8, dim)],
        ),
        out_shape=[
            jax.ShapeDtypeStruct((rows, dim), BF16),
            jax.ShapeDtypeStruct((2 * width, rows), BF16),
            jax.ShapeDtypeStruct((2 * width, rows), BF16),
            jax.ShapeDtypeStruct((8, dim), F32),
        ],
        cost_estimate=cost(8),
        name="norm_two",
    )(table, own, other, middle, grad_out, norms, *weights)


def first_total(dq_ref, dk_ref, dv_ref, w_ref):
    total = mm(dq_ref[...], w_ref[0])
    total = total + mm(dk_ref[...], w_ref[1])
    return total + mm(dv_ref[...], w_ref[2])


def first_grad_kernel(place_ref, dq_ref, dk_ref, dv_ref, w_ref, out_ref):
    out_ref[...] = first_total(dq_ref, dk_ref, dv_ref, w_ref).astype(BF16)


def first_grad(table, at, dq, dk, dv, weight):
    length, width = dq.shape
    dim = weight.shape[2]
    steps = length // BLK // 2
    rows = pl.BlockSpec((BLK, width), lambda i, p: (p[at] * steps + i, 0))
    return pl.pallas_call(
        first_grad_kernel,
        grid_spec=pltpu.PrefetchScalarGridSpec(
            num_scalar_prefetch=1,
            grid=(steps,),
            in_specs=[rows, rows, rows, pl.BlockSpec(weight.shape, lambda i, p: (0, 0, 0))],
            out_specs=pl.BlockSpec((BLK, dim), lambda i, p: (i, 0)),
        ),
        out_shape=jax.ShapeDtypeStruct((length // 2, dim), BF16),
        cost_estimate=cost(4),
        name="first_grad",
    )(table, dq, dk, dv, weight)


def norm_one_kernel(place_ref, dq_ref, dk_ref, dv_ref, w_ref, other_ref, x_ref, gm_ref, norm_ref, sums_two_ref,
                    out_ref, sums_ref):
    @pl.when(pl.program_id(0) == 0)
    def _():
        sums_ref[...] = sums_two_ref[...]
    g = first_total(dq_ref, dk_ref, dv_ref, w_ref) + other_ref[...].astype(F32)
    n, scale = normalized(x_ref[...].astype(F32))
    sums_ref[2:3, :] += jnp.sum(g * n, 0, keepdims=True)
    sums_ref[3:4, :] += jnp.sum(g, 0, keepdims=True)
    out_ref[...] = (gm_ref[...].astype(F32) + norm_back(g * norm_ref[0:1, :], n, scale)).astype(BF16)


def norm_one(table, dq, dk, dv, weight, other, tokens, gm, norms, sums_two):
    rows, dim = other.shape
    width = dq.shape[1]
    steps = rows // BLK
    local = pl.BlockSpec((BLK, dim), lambda i, p: (i, 0))
    placed = lambda d: pl.BlockSpec((BLK, d), lambda i, p: (p[MINE] * steps + i, 0))
    fixed = lambda *shape: pl.BlockSpec(shape, lambda i, p: (0,) * len(shape))
    return pl.pallas_call(
        norm_one_kernel,
        grid_spec=pltpu.PrefetchScalarGridSpec(
            num_scalar_prefetch=1,
            grid=(steps,),
            in_specs=[placed(width)] * 3 + [fixed(*weight.shape), local, placed(dim), local, fixed(*norms.shape),
                                            fixed(8, dim)],
            out_specs=[local, fixed(8, dim)],
        ),
        out_shape=[jax.ShapeDtypeStruct((rows, dim), BF16), jax.ShapeDtypeStruct((8, dim), F32)],
        cost_estimate=cost(10),
        name="norm_one",
    )(table, dq, dk, dv, weight, other, tokens, gm, norms, sums_two)


def fold_kernel(picks, cuts, table_ref, *refs):
    count = len(picks)
    ins, outs = refs[:2 * count], refs[2 * count:]
    for i in range(count):
        got, own = ins[2 * i], ins[2 * i + 1]
        base = table_ref[picks[i]] * got.shape[0]
        if cuts is None:
            at = pl.ds(pl.multiple_of(base, got.shape[0]), got.shape[0])
            outs[i][...] = (got[...].astype(F32) + own[at, :].astype(F32)).astype(BF16)
            continue
        keep, send = outs[2 * i], outs[2 * i + 1]
        rows = keep.shape[0]
        cut = table_ref[cuts[i]]
        for ref, half in ((keep, cut), (send, 1 - cut)):
            here = pl.ds(pl.multiple_of(half * rows, rows), rows)
            there = pl.ds(pl.multiple_of(base + half * rows, rows), rows)
            ref[...] = (got[here, :].astype(F32) + own[there, :].astype(F32)).astype(BF16)


def in_vmem(count):
    return [pl.BlockSpec(memory_space=VMEM)] * count


def fold(table, picks, cuts, pairs):
    outs, args = [], []
    for got, own in pairs:
        rows, dim = got.shape
        outs += [jax.ShapeDtypeStruct((rows, dim), BF16)] if cuts is None else [
            jax.ShapeDtypeStruct((rows // 2, dim), BF16)] * 2
        args += [got, own]
    res = pl.pallas_call(
        partial(fold_kernel, picks, cuts),
        in_specs=[pl.BlockSpec(memory_space=SMEM)] + in_vmem(len(args)),
        out_specs=in_vmem(len(outs)),
        out_shape=outs,
        cost_estimate=cost(1),
        name="fold",
    )(table, *args)
    return res if cuts is None else ([res[0], res[2]], [res[1], res[3]])


def join_kernel(bits, table_ref, *refs):
    count = len(bits)
    for i in range(count):
        own, got, out = refs[2 * i], refs[2 * i + 1], refs[2 * count + i]
        rows = own.shape[0]
        for ref, half in ((own, table_ref[bits[i]]), (got, 1 - table_ref[bits[i]])):
            out[pl.ds(pl.multiple_of(half * rows, rows), rows), :] = ref[...].astype(out.dtype)


def join(table, bits, pairs):
    outs, args = [], []
    for own, got in pairs:
        outs.append(jax.ShapeDtypeStruct((2 * own.shape[0], own.shape[1]), own.dtype))
        args += [own, got]
    return pl.pallas_call(
        partial(join_kernel, bits),
        in_specs=[pl.BlockSpec(memory_space=SMEM)] + in_vmem(len(args)),
        out_specs=in_vmem(len(outs)),
        out_shape=outs,
        cost_estimate=cost(1),
        name="join",
    )(table, *args)


def last_join_kernel(bits, table_ref, *refs):
    count = len(bits)
    for i in range(count):
        own, got, out = refs[2 * i], refs[2 * i + 1], refs[2 * count + i]
        for ref, half in ((own, table_ref[bits[i]]), (got, 1 - table_ref[bits[i]])):
            @pl.when(pl.program_id(0) == half)
            def _():
                out[...] = ref[...].astype(F32)


def last_join(table, bits, pairs):
    outs, specs, args = [], [], []
    for own, got in pairs:
        rows, dim = own.shape
        outs.append(jax.ShapeDtypeStruct((2 * rows, dim), F32))
        specs.append(pl.BlockSpec((rows, dim), lambda i: (i, 0)))
        args += [own, got]
    return pl.pallas_call(
        partial(last_join_kernel, bits),
        grid=(2,),
        in_specs=[pl.BlockSpec(memory_space=SMEM)] + in_vmem(len(args)),
        out_specs=specs,
        out_shape=outs,
        cost_estimate=cost(2),
        name="last_join",
    )(table, *args)


def dp_swap(value, distance):
    return lax.ppermute(value, "dp", [(d, d ^ distance) for d in range(lax.axis_size("dp"))])


ORDERS = ((0, 1, 2), (1, 2, 0))


def place_table():
    core = lax.axis_index("tensor") % 2
    code = lax.axis_index("dp") % 8 + 16 * core + 32 * (1 - core)
    return (code // jnp.array([1, 2, 4, 8, 16, 32, 64, 128], jnp.int32)) % 2


def dp_sum_pair(table, a, b, extra, held):
    if lax.axis_size("dp") != 8:
        a, b, extra = lax.psum((a, b, extra), "dp")
        return a.astype(F32), b.astype(F32), extra, held
    index = lax.axis_index("dp")
    rows = a.shape[0] // 2
    own = [a, b]
    send = [
        lax.dynamic_slice_in_dim(v, (1 - (index >> o[0]) % 2) * rows, rows, 0) for v, o in zip(own, ORDERS)
    ]
    for step in range(3):
        got = [dp_swap(v, 1 << o[step]) for v, o in zip(send, ORDERS)]
        extra = extra + dp_swap(extra, 1 << step)
        extra, got = lax.optimization_barrier((extra, got))
        picks = [o[0] if step == 0 else ZERO for o in ORDERS]
        pairs = list(zip(got, own))
        if step == 2:
            own = fold(table, picks, None, pairs)
            break
        own, send = fold(table, picks, [o[step + 1] for o in ORDERS], pairs)
    own, held = lax.optimization_barrier((own, held))
    for step in (2, 1, 0):
        got = [dp_swap(v, 1 << o[step]) for v, o in zip(own, ORDERS)]
        own = (join if step else last_join)(table, [o[step] for o in ORDERS], list(zip(own, got)))
    return *own, extra, held


def swap(value, distance):
    return lax.ppermute(value, "tensor", [(t, t ^ distance) for t in range(4)])


def add(a, b):
    return a.astype(F32) + b.astype(F32)


def both_halves(core, mine):
    other = swap(mine, 1)
    rows = mine.shape[0]
    full = jnp.zeros((2 * rows, mine.shape[1]), mine.dtype)
    full = lax.dynamic_update_slice(full, mine, (core * rows, 0))
    return lax.dynamic_update_slice(full, other, ((1 - core) * rows, 0))


def local(
    tokens,
    segment_ids,
    live_lengths,
    gain_one,
    shift_one,
    qkv_weight,
    out_weight,
    gain_two,
    shift_two,
    up_weight,
    down_weight,
    grad_out,
):
    core = lax.axis_index("tensor") % 2
    table = place_table()
    norms = jnp.stack([gain_one, shift_one, gain_two, shift_two])
    qkv = jnp.swapaxes(qkv_weight, 1, 2)
    w_far = swap(out_weight, 2)
    w_sib = swap(out_weight, 1)
    w_diag = swap(w_far, 1)

    first, q, k, v, info = front(live_lengths, segment_ids, tokens, norms, qkv)
    att, lse = attend(info, q, k, v)
    att, w_sib, w_far, w_diag = lax.optimization_barrier((att, w_sib, w_far, w_diag))
    weights = (out_weight, w_sib, w_far, w_diag)
    att_far = swap(att, 2)
    att_sib = swap(att, 1)
    att_diag = swap(att_far, 1)
    atts = (att, att_sib, att_far, att_diag)

    args = (atts, weights, tokens, grad_out, norms, up_weight, down_weight)
    second, hidden, grad_pre, out_theirs, gs_theirs, _ = middle_part(table, THEIRS, *args, ())
    gs_got = swap(gs_theirs, 1)
    second, hidden, grad_pre, out_mine, gs_mine, middle = middle_part(table, MINE, *args, (second, hidden, grad_pre))
    grad_mid, keep, send, sums_two = norm_two(table, gs_mine, gs_got, middle, grad_out, norms, weights)
    send, second, hidden, grad_pre = lax.optimization_barrier((send, second, hidden, grad_pre))
    got = swap(send, 2)
    width = out_weight.shape[0]
    out_half = add(out_mine, swap(out_theirs, 1)).astype(BF16)

    grad_down = jnp.einsum("tf,td->fd", hidden, grad_out, preferred_element_type=F32).astype(BF16)
    grad_up = jnp.einsum("td,tf->df", second, grad_pre, preferred_element_type=F32).astype(BF16)
    rows = tokens.shape[0] // 2
    pieces = [
        jnp.dot(lax.dynamic_slice_in_dim(a, core * rows, rows, 1), grad_mid, preferred_element_type=F32) for a in atts
    ]
    pieces = [p.astype(BF16) for p in pieces]
    own = add(pieces[0], swap(pieces[1], 1))
    far = add(pieces[2], swap(pieces[3], 1)).astype(BF16)

    got, out_half = lax.optimization_barrier((got, out_half))
    keep, grad_down, grad_up, own, far = lax.optimization_barrier((keep, grad_down, grad_up, own, far))
    far = swap(far, 2)
    out_far = swap(out_half, 2)
    grad_down, grad_up = (g.astype(F32) for g in lax.psum((grad_down, grad_up), "dp"))
    grad_att_own = add(keep[:width], got[:width]).astype(BF16)
    grad_att_sib = add(keep[width:], got[width:]).astype(BF16)
    grad_att_other = swap(grad_att_sib, 1)

    dq, dk, dv = attend_back(table, info, q, k, v, att, lse, grad_att_own, grad_att_other)
    dq, out_far = lax.optimization_barrier((dq, out_far))
    gf_got = swap(first_grad(table, THEIRS, dq, dk, dv, qkv), 1)
    partial_tokens, sums = norm_one(table, dq, dk, dv, qkv, gf_got, tokens, grad_mid, norms, sums_two)
    own, far, dq, dk, dv, partial_tokens = lax.optimization_barrier((own, far, dq, dk, dv, partial_tokens))
    grad_out_weight = (own + far.astype(F32)).astype(BF16)
    tokens_far = swap(partial_tokens, 2)
    output = both_halves(core, add(out_half, out_far).astype(BF16))
    sums = sums + swap(sums, 1)
    turn = lambda g: jnp.einsum("te,td->ed", g, first, preferred_element_type=F32).astype(BF16)
    grad_qk, grad_vo, sums, tokens_far = dp_sum_pair(
        table, jnp.concatenate([turn(dq), turn(dk)], 0), jnp.concatenate([turn(dv), grad_out_weight], 0), sums, tokens_far
    )
    sums, tokens_far = lax.optimization_barrier((sums, tokens_far))
    sums = sums + swap(sums, 2)
    grad_tokens = both_halves(core, add(partial_tokens, tokens_far).astype(BF16))
    grad_qkv = jnp.concatenate([grad_qk, grad_vo[:width]], 0).reshape(3, width, -1).swapaxes(1, 2)
    grad_out_weight = grad_vo[width:]
    return (
        output,
        grad_tokens,
        sums[2],
        sums[3],
        grad_qkv,
        grad_out_weight,
        sums[0],
        sums[1],
        grad_up,
        grad_down,
    )


def solution(mesh):
    in_specs = (
        P("dp", None),
        P("dp", None),
        P("dp"),
        P(),
        P(),
        P(None, None, "tensor"),
        P("tensor", None),
        P(),
        P(),
        P(None, "tensor"),
        P("tensor", None),
        P("dp", None),
    )
    out_specs = (
        P("dp", None),
        P("dp", None),
        P(),
        P(),
        P(None, None, "tensor"),
        P("tensor", None),
        P(),
        P(),
        P(None, "tensor"),
        P("tensor", None),
    )
    return jax.shard_map(local, mesh=mesh, in_specs=in_specs, out_specs=out_specs, check_vma=False)
```
